512 devices in a mesh: req: 64 (over x, y_hi, z), tp: 8 (over y_lo, core).
Axes of the slice: x: 4, y: 8 (y_hi: 2, y_lo: 4; y = y_hi * 4 + y_lo), z: 8, core: 2. Of those that a mesh axis runs over, the one named last changes fastest.
Arguments:
- states: bfloat16 [64, 256, 1536], P('req', 'tp'), may hold values from -7 to 7
- gain_attn: bfloat16 [1536], replicated, may hold values from 0.25 to 1.75
- gain_moe: bfloat16 [1536], replicated, may hold values from 0.25 to 1.75
- w_query: bfloat16 [1536, 1536], P(None, 'tp'), may hold values from -4 to 4
- w_keyval: bfloat16 [1536, 1024], P(None, 'tp'), may hold values from -4 to 4
- w_out: bfloat16 [1536, 1536], P('tp'), may hold values from -0.875 to 0.875
- prefix_cache: bfloat16 [64, 128, 1024], P('req', None, 'tp'), may hold values from -6 to 6
- w_gate_up: bfloat16 [64, 1536, 512], P('req'), may hold values from -0.15625 to 0.15625
- w_down: bfloat16 [64, 256, 1536], P('req'), may hold values from -0.25 to 0.25
- routes: int32 [64, 256, 8], P('req', 'tp'), may hold values from 0 to 31, all different within a row; in each aligned block of 32 rows (0 to 31, 32 to 63, ..., all dimensions but the last counted through in order) at most 10 rows name the same one
- gates: float32 [64, 256, 8], P('req', 'tp'), may hold values from 0.05 to 0.3
- lengths: int32 [64], replicated, may hold values from 1 to 256, 14336 in all
- group_of: int32 [64], replicated, may hold values from 0 to 15
- owners: int32 [64], replicated, may hold values from 0 to 63, each once
Outputs:
- layer_out: bfloat16 [64, 256, 1536], P('req', 'tp')
The draws below stay inside these ranges and needn't reach their ends.
Inputs may be any that keep to these rules, and one draw needn't show every extreme that they name: `routes`: in each aligned block of 32 rows (all leading dimensions taken together, in order) no expert is named by more than 10 rows, a bound that some block reaches. `owners`: each index of req appears once.
All inputs are finite; a program needn't handle non-finite values.
Results may differ from the reference program's by a relative error of at most 0.02.
Values may be sent and summed in bfloat16 or wider, within the bound.
No kernel may reach another device: no remote copies, remote signals or barrier semaphores. Data moves between devices by JAX's collectives and lax.ppermute only.
A program may use at most 64 MiB of HBM per device.

```python
import math
import jax
import jax.numpy as jnp
import numpy as np
from jax import lax

D = 1536
QH = 24
KVH = 8
HD = 64
FF = 512
EXPERTS = 32
TOPK = 8
PIECES = 4
SMAX = 256
PSEG = 128
HALF = 256
REQS = 64
GROUPS = 16
ROWS_TP = 32
CAP = 10
N_REQ = 64
N_TP = 8


def query_base(key):
    return jax.random.truncated_normal(jax.random.fold_in(key, 101), -6.0, 6.0, (D, QH * HD), jnp.float32) * D ** (-0.5)


def draw_states(key, part):
    base = jax.random.truncated_normal(jax.random.fold_in(key, 404), -6.0, 6.0, (REQS, SMAX, D), jnp.float32)
    return jnp.clip(base, -6.5, 6.5).astype(jnp.bfloat16)


def draw_w_query(key, part):
    base = query_base(key)
    return jnp.clip(base, -4.0, 4.0).astype(jnp.bfloat16)


def draw_w_keyval(key, part):
    drawn = jax.random.truncated_normal(jax.random.fold_in(key, 303), -6.0, 6.0, (D, KVH, 2, HD), jnp.float32) * D ** (-0.5)
    return jnp.clip(drawn.reshape(D, KVH * 2 * HD), -4.0, 4.0).astype(jnp.bfloat16)


def plant(array, stream_key, least, high):
    dims = array.shape
    spot = [jax.random.randint(jax.random.fold_in(stream_key, axis), (), 0, dims[axis]) for axis in range(len(dims))]
    array = array.at[tuple(spot)].set(least)
    longest = dims.index(max(dims))
    spot[longest] = (spot[longest] + 1) % dims[longest]
    return array.at[tuple(spot)].set(high)


def block_scale(stream_key, dims, cuts, least, largest):
    loudness, own = 1.0, jax.random.fold_in(stream_key, 6)
    for axis_at, blocks in cuts:
        draws = jnp.exp(jax.random.uniform(jax.random.fold_in(own, axis_at), (blocks,), jnp.float32, least / len(cuts), largest / len(cuts)))
        loudness = loudness * jnp.repeat(draws, dims[axis_at] // blocks).reshape([-1 if axis == axis_at else 1 for axis in range(len(dims))])
    return loudness


def split_up(number_of, total, bound, skew):
    loads = [(1 << 20) // math.isqrt(standing ** skew) + 1 for standing in range(2, number_of + 1)]
    surplus, holding = total - bound - (number_of - 1), [1] * (number_of - 1)
    while surplus > 0:
        free = [i for i in range(number_of - 1) if holding[i] < bound]
        pool, left = sum([loads[i] for i in free]), surplus
        for i in free:
            addition = min(bound - holding[i], max(1, left * loads[i] // pool), surplus)
            holding[i] = holding[i] + addition
            surplus = surplus - addition
    return np.array([bound] + holding)


def ragged(rng, count, total, reach, slope):
    if count == 2:
        one = jax.random.randint(rng, (), max(1, total - reach), min(reach, total - 1) + 1)
        return jnp.stack([one, total - one])
    sizes = jnp.asarray(split_up(count, total, reach, slope), jnp.int32)
    couples = (count - 1) // 2
    source_of, taker = sizes[1:1 + 2 * couples:2], sizes[2:2 + 2 * couples:2]
    slack = jnp.minimum(source_of - 1, reach - taker)
    passed = jax.random.randint(jax.random.fold_in(rng, 1), (couples,), 0, 1 << 20) % (slack + 1)
    sizes = sizes.at[1:1 + 2 * couples:2].set(source_of - passed).at[2:2 + 2 * couples:2].set(taker + passed)
    return sizes[jax.random.permutation(jax.random.fold_in(rng, 2), count)]


def routed_block(own_key, own, number, rows, count, top, reach, slope):
    ranking = jax.random.permutation(own_key, count)
    packed, usual = load_shares(count, rows * top, reach, slope, True), load_shares(count, rows * top, reach, slope, False)
    places = jnp.arange(count)

    def named(tallies, turn):
        used = int((tallies > 0).sum())
        fixed = max(1, used // 4)
        passed = fixed + (places - fixed + turn * (used - fixed)) % max(1, count - fixed)
        return jnp.zeros((count,), jnp.int32).at[ranking[jnp.where(places < fixed, places, passed)]].set(jnp.asarray(tallies, jnp.int32))

    tallies = jnp.where(number % 4 == 0, named(packed, number // 4), named(usual, number - number // 4 - 1))
    mixed = jax.random.permutation(jax.random.fold_in(own, 3), count)
    donor, receiver = mixed[0:count // 2 * 2:2], mixed[1:count // 2 * 2:2]
    margin = jnp.minimum(tallies[donor] - 1, reach - tallies[receiver]) // 2
    margin = jnp.where((donor == ranking[0]) | (receiver == ranking[0]) | (tallies[receiver] == 0), 0, jnp.maximum(margin, 0))
    passed = jax.random.randint(jax.random.fold_in(own, 4), (count // 2,), 0, 1 << 20) % (margin + 1)
    tallies = tallies.at[donor].add(-passed).at[receiver].add(passed)
    members = jnp.searchsorted(jnp.cumsum(tallies), jnp.arange(rows * top), side="right").astype(jnp.int32)
    grid = members.reshape(top, rows).T
    grid = grid[jax.random.permutation(jax.random.fold_in(own, 1), rows)]
    turn = jax.random.randint(jax.random.fold_in(own, 2), (rows, 1), 0, top)
    return jnp.take_along_axis(grid, (jnp.arange(top)[None, :] + turn) % top, axis=1)


def load_shares(number_of, total, reach, slope, full):
    weights = [(1 << 20) // math.isqrt(grade ** slope) + 1 for grade in range(1, number_of + 1)]
    largest = reach if full else min(reach, max(-(-total // number_of), total * weights[0] // sum(weights)))
    least = 1 if total - largest >= number_of - 1 else 0
    counts, spare = [largest] + [least] * (number_of - 1), total - largest - least * (number_of - 1)
    while spare > 0:
        movable = [i for i in range(1, number_of) if counts[i] < largest] or [i for i in range(1, number_of) if counts[i] < reach]
        mass, left = sum([weights[i] for i in movable]), spare
        for i in movable:
            extra = min(reach - counts[i], max(1, left * weights[i] // mass), spare)
            counts[i] = counts[i] + extra
            spare = spare - extra
    return np.array(counts)


def scatter_about(rng, dims, scale, bound, split=(), held_as=jnp.bfloat16):
    entries = scale * jax.random.normal(rng, dims, jnp.float32)
    if split:
        entries = entries * block_scale(rng, dims, split, -0.22, 0.18)
    return jnp.clip(entries, -bound, bound).astype(held_as)


def setup_inputs(seed: int = 0) -> dict:
    key_of = jax.random.split(jax.random.key(seed), 15)
    states = draw_states(jax.random.fold_in(key_of[14], 71), 0)
    gain_attn = jnp.clip(1.0 + 0.15 * jax.random.normal(key_of[1], (D,), jnp.float32), 0.25, 1.75).astype(jnp.bfloat16)
    gain_moe = jnp.clip(1.0 + 0.15 * jax.random.normal(key_of[2], (D,), jnp.float32), 0.25, 1.75).astype(jnp.bfloat16)
    w_query = draw_w_query(jax.random.fold_in(key_of[14], 71), 0)
    w_keyval = draw_w_keyval(jax.random.fold_in(key_of[14], 71), 0)
    w_out = scatter_about(key_of[5], (QH * HD, D), (QH * HD // 32) ** -0.5, 0.875, ((0, 8),))
    prefix_cache = scatter_about(key_of[6], (N_REQ, PSEG, KVH * 2 * HD), 1.0, 6.0, ((0, 64), (2, 8)))
    w_gate_up = scatter_about(key_of[7], (2 * EXPERTS, D, FF), D ** -0.5, 0.15625, ((0, 64),))
    w_down = scatter_about(key_of[8], (2 * EXPERTS, HALF, D), FF ** -0.5, 0.25, ((0, 64),))
    routes_keys = jax.random.split(jax.random.fold_in(key_of[9], 1), REQS * SMAX // ROWS_TP)
    routes_turns = jax.random.permutation(jax.random.fold_in(key_of[9], 3), REQS * SMAX // ROWS_TP)
    routes = jax.vmap(lambda own, number: routed_block(jax.random.fold_in(key_of[9], 2), own, number, ROWS_TP, EXPERTS, TOPK, CAP, 2))(routes_keys, routes_turns).reshape((REQS, SMAX, TOPK))
    gates = jnp.clip(0.05 + 0.25 * jax.random.uniform(key_of[10], (REQS, SMAX, TOPK), jnp.float32) ** block_scale(key_of[10], (REQS, SMAX, TOPK), ((0, 64), (1, 8)), -0.2, 0.2), 0.05, 0.3)
    lengths = ragged(key_of[11], REQS, 7 * SMAX // 8 * REQS, SMAX, 2).astype(jnp.int32)
    group_of = plant(jax.random.randint(key_of[12], (REQS,), 0, GROUPS), jax.random.fold_in(key_of[12], 1), 0, GROUPS - 1).astype(jnp.int32)
    owners = jax.random.permutation(key_of[13], N_REQ).astype(jnp.int32)
    return dict(states=states, gain_attn=gain_attn, gain_moe=gain_moe, w_query=w_query, w_keyval=w_keyval, w_out=w_out, prefix_cache=prefix_cache, w_gate_up=w_gate_up, w_down=w_down, routes=routes, gates=gates, lengths=lengths, group_of=group_of, owners=owners)


def rms_scale(values, gain):
    values = values.astype(jnp.float32)
    spread = lax.rsqrt(lax.optimization_barrier(jnp.mean(values * values, axis=-1, keepdims=True)) + 1e-05)
    return values * spread * gain.astype(jnp.float32)

def apply_rotary(tensor, offset):
    count = tensor.shape[0]
    width = tensor.shape[-1] // 2
    place = offset + jnp.arange(count, dtype=jnp.float32)
    freq = jnp.exp(jnp.arange(width, dtype=jnp.float32) * (-2.0 * math.log(10000.0) / tensor.shape[-1]))
    angle = place[:, None] * freq[None, :]
    cosine = jnp.cos(angle)[:, None, :]
    sine = jnp.sin(angle)[:, None, :]
    first = tensor[..., :width]
    second = tensor[..., width:]
    return jnp.concatenate([first * cosine - second * sine, second * cosine + first * sine], axis=-1)

def reference(states, gain_attn, gain_moe, w_query, w_keyval, w_out, prefix_cache, w_gate_up, w_down, routes, gates, lengths, group_of, owners):
    per_kv = QH // KVH
    plen = PIECES * PSEG
    normed = rms_scale(states, gain_attn).astype(jnp.bfloat16)

    def attend(index):
        rows = normed[index]
        group = group_of[index]
        length = lengths[index]
        query_rows = jnp.dot(rows, w_query, preferred_element_type=jnp.float32).reshape(SMAX, QH, HD)
        query_rows = apply_rotary(query_rows, plen).astype(jnp.bfloat16)
        keyvals = jnp.dot(rows, w_keyval, preferred_element_type=jnp.float32).reshape(SMAX, KVH, 2, HD)
        keys = apply_rotary(keyvals[:, :, 0], plen).astype(jnp.bfloat16)
        values = keyvals[:, :, 1].astype(jnp.bfloat16)
        holders = lax.dynamic_slice(owners, ((group * PIECES).astype(jnp.int32),), (PIECES,))
        pieces = prefix_cache[holders].reshape(plen, KVH, 2, HD)
        all_keys = jnp.concatenate([pieces[:, :, 0], keys], axis=0).astype(jnp.float32)
        all_values = jnp.concatenate([pieces[:, :, 1], values], axis=0).astype(jnp.float32)
        grouped = query_rows.reshape(SMAX, KVH, per_kv, HD).astype(jnp.float32)
        scores = jnp.einsum('ihrd,jhd->hrij', grouped, all_keys) * (1.0 / math.sqrt(HD))
        query_position = jnp.arange(SMAX)[:, None]
        key_at = jnp.arange(plen + SMAX)[None, :] - plen
        visible = (key_at < 0) | (key_at <= query_position) & (key_at < length)
        scores = jnp.where(visible, scores, -1e+30)
        top = lax.optimization_barrier(jnp.max(scores, axis=-1, keepdims=True))
        weights = jnp.where(visible, jnp.exp(scores - top), 0.0)
        total = lax.optimization_barrier(jnp.sum(weights, axis=-1))
        rounded_length = lax.optimization_barrier(weights.astype(jnp.bfloat16)).astype(jnp.float32)
        mixed = jnp.einsum('hrij,jhd->ihrd', rounded_length, all_values)
        mixed = mixed / jnp.transpose(total, (2, 0, 1))[..., None]
        attn = mixed.reshape(SMAX, QH * HD).astype(jnp.bfloat16)
        return states[index].astype(jnp.float32) + jnp.dot(attn, w_out, preferred_element_type=jnp.float32)
    residual = lax.map(attend, jnp.arange(REQS))
    n_rows = REQS * SMAX
    normed_moe = rms_scale(residual, gain_moe).astype(jnp.bfloat16).reshape(n_rows, D)
    rows_per_tensor_shard = SMAX // N_TP
    blocks = n_rows // rows_per_tensor_shard
    count = rows_per_tensor_shard * TOPK
    chosen = routes.reshape(blocks, count)
    onehot = (chosen[..., None] == jnp.arange(EXPERTS)[None, None, :]).astype(jnp.int32)
    slot_in = lax.optimization_barrier(jnp.sum(jnp.cumsum(onehot, axis=1) * onehot, axis=-1)) - 1
    line = (jnp.arange(blocks)[:, None] * CAP + slot_in).reshape(-1)
    expert = chosen.reshape(-1)
    source = (jnp.arange(blocks * count) // TOPK).astype(jnp.int32)
    table = jnp.full((EXPERTS, blocks * CAP), n_rows, jnp.int32).at[expert, line].set(source)
    weight_table = jnp.zeros((EXPERTS, blocks * CAP), jnp.float32).at[expert, line].set(gates.reshape(-1).astype(jnp.float32))
    padded = jnp.concatenate([normed_moe, jnp.zeros((1, D), jnp.bfloat16)], axis=0)

    def expert_step(mixed_sum, expert_index):
        take = padded[table[expert_index]]
        result = jnp.zeros((blocks * CAP, D), jnp.float32)
        for half in range(2):
            slot = 2 * expert_index + half
            pair = jnp.dot(take, w_gate_up[slot], preferred_element_type=jnp.float32)
            inner = (jax.nn.silu(pair[:, :HALF]) * pair[:, HALF:]).astype(jnp.bfloat16)
            part = jnp.dot(inner, w_down[slot], preferred_element_type=jnp.float32).astype(jnp.bfloat16)
            result = result + part.astype(jnp.float32)
        mixed_sum = mixed_sum.at[table[expert_index]].add(weight_table[expert_index][:, None] * result, mode='drop')
        return (mixed_sum, None)
    expert_blend, unused = lax.scan(expert_step, jnp.zeros((n_rows, D), jnp.float32), jnp.arange(EXPERTS))
    final = residual + expert_blend.reshape(REQS, SMAX, D)
    live = jnp.arange(SMAX)[None, :, None] < lengths[:, None, None]
    return jnp.where(live, final, 0.0).astype(jnp.bfloat16)
```

```python
import functools
import math

import jax
import jax.numpy as jnp
import numpy as np
from jax import lax
from jax.experimental import pallas as pl
from jax.experimental.pallas import tpu as pltpu
from jax.sharding import Mesh, PartitionSpec as P

D = 1536
HD = 64
EXPERTS = 32
TOPK = 8
PIECES = 4
CAP = 10
MAIN = 8
REM = CAP - MAIN
ROWS = 32
CHUNKS = D // 128
UNITS = CAP * CHUNKS
PLEN = 512
SMAX = 256
F32 = jnp.float32
BF16 = jnp.bfloat16

VM = pl.BlockSpec(memory_space=pltpu.VMEM)
SM = pl.BlockSpec(memory_space=pltpu.SMEM)


def call(body, outs, n_in, smem=(), scratch=()):
    single = not isinstance(outs, (list, tuple))
    return pl.pallas_call(
        body,
        out_shape=outs,
        in_specs=[SM if i in smem else VM for i in range(n_in)],
        out_specs=VM if single else [VM] * len(outs),
        scratch_shapes=list(scratch),
    )


def dot(a, b):
    return jnp.dot(a, b, preferred_element_type=F32)


def iota(shape, dim):
    return lax.broadcasted_iota(jnp.int32, shape, dim)


def ones_where(cond, dtype=BF16):
    return jnp.where(cond, 1.0, 0.0).astype(dtype)


def rotary_tables():
    place = np.float32(PLEN) + np.arange(SMAX, dtype=np.float32)
    freq = np.exp(
        np.arange(HD // 2, dtype=np.float32) * np.float32(-2.0 * math.log(10000.0) / HD)
    ).astype(np.float32)
    angle = (place[:, None] * freq[None, :]).astype(np.float32).astype(np.float64)
    cosine, sine = np.cos(angle), np.sin(angle)
    one, zero = np.ones((SMAX, HD)), np.zeros((SMAX, HD))
    return (
        np.concatenate([cosine, cosine, one], axis=1).astype(np.float32),
        np.concatenate([sine, sine, zero], axis=1).astype(np.float32),
    )


def rms(values, gain):
    spread = lax.rsqrt(jnp.mean(values * values, axis=-1, keepdims=True) + 1e-05)
    return values * spread * gain


def norm_body(states, gain, out):
    out[...] = rms(states[...].astype(F32), gain[...].astype(F32)).astype(BF16)


def select_body(meta, owners, group_of, held, out):
    base = meta[0]
    for z in range(8):
        group = group_of[base + z]
        for j in range(PIECES):
            out[z, j] = held[owners[group * PIECES + j]]


def qkv_body(rows, w_query, w_keyval, cosine, sine, q_out, kv_out):
    x = rows[...]
    wq = w_query[...]
    wkv = w_keyval[...]
    src, dst = iota((192, 128), 0), iota((192, 128), 1)
    ksrc, kdst = iota((128, 128), 0), iota((128, 128), 1)

    def turned(source, target, base):
        first = (target < 32) & (source == base + target + 32)
        second = (target >= 32) & (target < 64) & (source == base + target - 32)
        return jnp.where(first, -1.0, jnp.where(second, 1.0, 0.0)).astype(BF16)

    cos, sin = cosine[...], sine[...]
    for h in range(3):
        plain = ones_where((dst < HD) & (src == h * HD + dst))
        straight = dot(x, dot(wq, plain).astype(BF16))
        crossed = dot(x, dot(wq, turned(src, dst, h * HD)).astype(BF16))
        q_out[pl.ds(h * SMAX, SMAX), :] = (straight * cos + crossed * sin).astype(BF16)
    straight = dot(x, wkv)
    crossed = dot(x, dot(wkv, turned(ksrc, kdst, 0)).astype(BF16))
    kv_out[...] = (straight * cos + crossed * sin).astype(BF16)


def attend_body(meta, q_ref, kv_ref, prefix_ref, w_out, mine_out, other_out):
    length, core = meta[0], meta[1]
    kv = kv_ref[...]
    prefix = prefix_ref[...]
    dims = (((1,), (1,)), ((), ()))
    key_at = iota((SMAX, SMAX), 1)
    keep = (key_at <= iota((SMAX, SMAX), 0)) & (key_at < length)
    heads = []
    for h in range(3):
        q = q_ref[pl.ds(h * SMAX, SMAX), :]
        far = lax.dot_general(q, prefix, dims, preferred_element_type=F32) * 0.125
        near = lax.dot_general(q, kv, dims, preferred_element_type=F32) * 0.125
        near = jnp.where(keep, near, -1e30)
        top = jnp.maximum(
            jnp.max(far, axis=-1, keepdims=True), jnp.max(near, axis=-1, keepdims=True)
        )
        far = jnp.exp(far - top)
        near = jnp.where(keep, jnp.exp(near - top), 0.0)
        total = jnp.sum(far, axis=-1, keepdims=True) + jnp.sum(near, axis=-1, keepdims=True)
        mixed = dot(far.astype(BF16), prefix) + dot(near.astype(BF16), kv)
        heads.append((mixed / total)[:, HD:].astype(BF16))
    partial = dot(jnp.concatenate(heads, axis=1), w_out[...])
    partial = partial.reshape(4, 2, ROWS, D)
    first = core == 0
    mine_out[...] = jnp.where(first, partial[:, 0], partial[:, 1])
    other_out[...] = jnp.where(first, partial[:, 1], partial[:, 0]).astype(BF16)


def add_body(a, b, out):
    out[...] = (a[...] + b[...].astype(F32)).astype(BF16)


def shuffle_matrix(transposed):
    n = 4 * REM * CHUNKS
    i = iota((n, n), 1 if transposed else 0)
    j = iota((n, n), 0 if transposed else 1)
    per = REM * CHUNKS
    same = (i % (4 * REM)) // REM == j // per
    return ones_where(same & (j % per == REM * (i // (4 * REM)) + i % REM))


def pack(main, rest, out):
    for c in range(CHUNKS):
        part = main[:, c * 128 : (c + 1) * 128].reshape(EXPERTS, MAIN, 128)
        out[:, c * MAIN : (c + 1) * MAIN, :] = part.astype(BF16)
    shuffle = shuffle_matrix(True)
    for g in range(EXPERTS // 4):
        block = rest[g * 8 : (g + 1) * 8, :]
        stacked = jnp.concatenate(
            [block[:, c * 128 : (c + 1) * 128] for c in range(CHUNKS)], axis=0
        ).astype(BF16)
        units = dot(shuffle, stacked).reshape(4, REM * CHUNKS, 128)
        out[g * 4 : (g + 1) * 4, CHUNKS * MAIN :, :] = units.astype(BF16)


def unpack(units_ref, rows_ref):
    for c in range(CHUNKS):
        part = units_ref[:, c * MAIN : (c + 1) * MAIN, :].astype(F32)
        rows_ref[0 : EXPERTS * MAIN, c * 128 : (c + 1) * 128] = part.reshape(
            EXPERTS * MAIN, 128
        ).astype(BF16)
    shuffle = shuffle_matrix(False)
    gathered = []
    for g in range(EXPERTS // 4):
        units = units_ref[g * 4 : (g + 1) * 4, CHUNKS * MAIN :, :].astype(F32)
        gathered.append(dot(shuffle, units.reshape(4 * REM * CHUNKS, 128).astype(BF16)))
    for c in range(CHUNKS):
        part = jnp.concatenate([rows[c * 8 : (c + 1) * 8] for rows in gathered], axis=0)
        rows_ref[EXPERTS * MAIN :, c * 128 : (c + 1) * 128] = part.astype(BF16)


def place_of(index):
    expert = jnp.where(index < EXPERTS * MAIN, index // MAIN, (index - EXPERTS * MAIN) // REM)
    turn = jnp.where(index < EXPERTS * MAIN, index % MAIN, MAIN + index % REM)
    return expert, turn


def dispatch_body(parts, states, gain, routes_t, resid_out, out):
    residual = states[...].astype(F32) + jnp.sum(parts[...].astype(F32), axis=0)
    resid_out[...] = residual
    normed = rms(residual, gain[...].astype(F32)).astype(BF16)
    expert = iota((EXPERTS, ROWS), 0)
    named = jnp.zeros((EXPERTS, ROWS), F32)
    for k in range(TOPK):
        named = named + ones_where(routes_t[k : k + 1, :] == expert, F32)
    named = named.astype(BF16)
    earlier = ones_where(iota((ROWS, ROWS), 0) < iota((ROWS, ROWS), 1))
    turn_of = dot(named, earlier).astype(BF16)
    total = EXPERTS * CAP
    owner, turn = place_of(iota((total, EXPERTS), 0))
    spread = ones_where(owner == iota((total, EXPERTS), 1))
    turn = turn[:, :1].astype(F32)
    pick = ones_where((dot(spread, named) > 0.5) & (dot(spread, turn_of) == turn))
    sent = dot(pick, normed)
    pack(sent[: EXPERTS * MAIN], sent[EXPERTS * MAIN :], out)


def expert_body(units, gate_up_a, gate_up_b, down_a, down_b, out, rows):
    unpack(units, rows)
    x = rows[...]
    half = 256
    result = None
    for gate_up, down in ((gate_up_a, down_a), (gate_up_b, down_b)):
        pair = dot(x, gate_up[...])
        gate = pair[:, :half]
        inner = (gate * jax.nn.sigmoid(gate) * pair[:, half:]).astype(BF16)
        part = dot(inner, down[...])
        result = part if result is None else result + part
    pack(result[: EXPERTS * MAIN], result[EXPERTS * MAIN :], out)


def combine_body(meta, units, routes, gates, residual, out, rows):
    length, first = meta[0], meta[1]
    unpack(units, rows)
    expert = iota((ROWS, EXPERTS), 1)
    named = jnp.zeros((ROWS, EXPERTS), F32)
    weight = jnp.zeros((ROWS, EXPERTS), F32)
    for k in range(TOPK):
        hit = routes[:, k : k + 1] == expert
        named = jnp.where(hit, 1.0, named)
        weight = jnp.where(hit, gates[:, k : k + 1], weight)
    named = named.astype(BF16)
    earlier = ones_where(iota((ROWS, ROWS), 1) < iota((ROWS, ROWS), 0))
    turn_of = dot(earlier, named).astype(BF16)
    total = EXPERTS * CAP
    owner, turn = place_of(iota((EXPERTS, total), 1))
    spread = ones_where(owner == iota((EXPERTS, total), 0))
    turn = turn[:1, :].astype(F32)
    pick = (dot(named, spread) > 0.5) & (dot(turn_of, spread) == turn)
    high = weight.astype(BF16)
    left = weight - high.astype(F32)
    middle = left.astype(BF16)
    low = (left - middle.astype(F32)).astype(BF16)
    terms = [
        jnp.where(pick, dot(term, spread), 0.0).astype(BF16) for term in (low, middle, high)
    ]
    data = rows[...]
    blend = dot(terms[0], data) + dot(terms[1], data) + dot(terms[2], data)
    live = first + iota((ROWS, 1), 0) < length
    out[...] = jnp.where(live, residual[...] + blend, 0.0).astype(BF16)


def on_device(
    states,
    gain_attn,
    gain_moe,
    w_query,
    w_keyval,
    w_out,
    prefix_cache,
    w_gate_up,
    w_down,
    routes,
    gates,
    lengths,
    group_of,
    owners,
):
    lane = lax.axis_index(("x", "yh", "z1", "z0"))
    core = lax.axis_index("c")
    column = lax.axis_index(("l1", "l0", "c"))
    length = lengths[lane]
    local = states[0]
    cosine, sine = rotary_tables()
    shape = jax.ShapeDtypeStruct

    with jax.named_scope("prefix_slices"):
        slices = prefix_cache[0].reshape(1, 8, 16, 128)
        slices = jnp.broadcast_to(slices, (8, 8, 16, 128)).reshape(64, 16, 128)
        held = lax.all_to_all(slices, ("x", "yh", "z1", "z0"), 0, 0, tiled=True)
    with jax.named_scope("norm_attn"):
        normed = call(norm_body, shape((ROWS, D), BF16), 2)(local, gain_attn[None])
        gathered = lax.all_gather(normed, ("l1", "l0", "c"), axis=0, tiled=True)
    with jax.named_scope("prefix_deliver"):
        base = ((lane // 8) * 8).astype(jnp.int32)[None]
        chosen = call(select_body, shape((8, PIECES, 16, 128), BF16), 4, smem=(0, 1, 2))(
            base, owners, group_of, held
        )
        prefix = lax.all_to_all(chosen, ("z1", "z0"), 0, 0, tiled=True).reshape(PLEN, 128)
    with jax.named_scope("expert_swap"):
        swap = [(0, 1), (1, 0)]
        gate_up_b = lax.ppermute(w_gate_up, "z0", swap)
        down_b = lax.ppermute(w_down, "z0", swap)
    with jax.named_scope("project"):
        queries, keyvals = call(
            qkv_body, (shape((3 * SMAX, 128), BF16), shape((SMAX, 128), BF16)), 5
        )(gathered, w_query, w_keyval, cosine, sine)
    with jax.named_scope("attend"):
        meta = jnp.stack([length, core.astype(jnp.int32)])
        mine, other = call(
            attend_body,
            (shape((4, ROWS, D), F32), shape((4, ROWS, D), BF16)),
            5,
            smem=(0,),
        )(meta, queries, keyvals, prefix, w_out)
    with jax.named_scope("sum_heads"):
        other = lax.ppermute(other, "c", [(0, 1), (1, 0)])
        both = call(add_body, shape((4, ROWS, D), BF16), 2)(mine, other)
        parts = lax.all_to_all(both, ("l1", "l0"), 0, 0, tiled=True)
    with jax.named_scope("dispatch"):
        residual, outbound = call(
            dispatch_body,
            (shape((ROWS, D), F32), shape((EXPERTS, UNITS, 128), BF16)),
            4,
        )(parts, local, gain_moe[None], routes[0].T)
        inbound = lax.all_to_all(outbound, ("x", "yh", "z1"), 0, 0, tiled=True)
    with jax.named_scope("experts"):
        produced = call(
            expert_body,
            shape((EXPERTS, UNITS, 128), BF16),
            5,
            scratch=(pltpu.VMEM((EXPERTS * CAP, D), BF16),),
        )(inbound, w_gate_up[0], gate_up_b[0], w_down[0], down_b[0])
        returned = lax.all_to_all(produced, ("x", "yh", "z1"), 0, 0, tiled=True)
    with jax.named_scope("combine"):
        meta = jnp.stack([length, (column * ROWS).astype(jnp.int32)])
        final = call(
            combine_body,
            shape((ROWS, D), BF16),
            5,
            smem=(0,),
            scratch=(pltpu.VMEM((EXPERTS * CAP, D), BF16),),
        )(meta, returned, routes[0], gates[0], residual)
    return final[None]


def solution(mesh):
    fine = Mesh(
        mesh.devices.reshape(4, 2, 4, 2, 2, 2, 2), ("x", "yh", "z1", "z0", "l1", "l0", "c")
    )
    req, tp = ("x", "yh", "z1", "z0"), ("l1", "l0", "c")
    placed = (
        P(req, tp, None),
        P(),
        P(),
        P(None, tp),
        P(None, tp),
        P(tp, None),
        P(req, None, tp),
        P(req, None, None),
        P(req, None, None),
        P(req, tp, None),
        P(req, tp, None),
        P(),
        P(),
        P(),
    )
    return jax.shard_map(
        on_device, mesh=fine, in_specs=placed, out_specs=P(req, tp, None), check_vma=False
    )
```

```python
import math

import jax
import jax.numpy as jnp
import numpy as np
from jax import lax
from jax.experimental import pallas as pl
from jax.experimental.pallas import tpu as pltpu
from jax.sharding import Mesh, PartitionSpec as P

D = 1536
HD = 64
EXPERTS = 32
TOPK = 8
PIECES = 4
CAP = 10
MAIN = 8
REM = CAP - MAIN
ROWS = 32
CHUNKS = D // 128
UNITS = CAP * CHUNKS
PLEN = 512
SMAX = 256
F32 = jnp.float32
BF16 = jnp.bfloat16

VM = pl.BlockSpec(memory_space=pltpu.VMEM)
SM = pl.BlockSpec(memory_space=pltpu.SMEM)


def call(body, outs, n_in, smem=(), scratch=()):
    single = not isinstance(outs, (list, tuple))
    return pl.pallas_call(
        body,
        out_shape=outs,
        in_specs=[SM if i in smem else VM for i in range(n_in)],
        out_specs=VM if single else [VM] * len(outs),
        scratch_shapes=list(scratch),
    )


def dot(a, b):
    return jnp.dot(a, b, preferred_element_type=F32)


def iota(shape, dim):
    return lax.broadcasted_iota(jnp.int32, shape, dim)


def ones_where(cond, dtype=BF16):
    return jnp.where(cond, 1.0, 0.0).astype(dtype)


def rotary_tables():
    place = np.float32(PLEN) + np.arange(SMAX, dtype=np.float32)
    freq = np.exp(
        np.arange(HD // 2, dtype=np.float32) * np.float32(-2.0 * math.log(10000.0) / HD)
    ).astype(np.float32)
    angle = (place[:, None] * freq[None, :]).astype(np.float32).astype(np.float64)
    cosine, sine = np.cos(angle), np.sin(angle)
    one, zero = np.ones((SMAX, HD)), np.zeros((SMAX, HD))
    return (
        np.concatenate([cosine, cosine, one], axis=1).astype(np.float32),
        np.concatenate([sine, sine, zero], axis=1).astype(np.float32),
    )


def rms(values, gain):
    spread = lax.rsqrt(jnp.mean(values * values, axis=-1, keepdims=True) + 1e-05)
    return values * spread * gain


def norm_body(states, gain, out):
    out[...] = rms(states[...].astype(F32), gain[...].astype(F32)[None]).astype(BF16)


def select_body(base_ref, owners, group_of, held, out):
    base = base_ref[0]
    for z in range(8):
        group = group_of[base + z]
        for j in range(PIECES):
            out[z, j] = held[owners[group * PIECES + j]]


def dot_t(a, b):
    return lax.dot_general(a, b, (((1,), (1,)), ((), ())), preferred_element_type=F32)


def qkv_body(rows, w_query_t, w_keyval, cosine, sine, q_out, kv_out):
    x = rows[...]
    wq = w_query_t[...]
    wkv = w_keyval[...]
    src, dst = iota((128, 192), 1), iota((128, 192), 0)
    ksrc, kdst = iota((128, 128), 0), iota((128, 128), 1)

    def turned(source, target, base):
        first = (target < 32) & (source == base + target + 32)
        second = (target >= 32) & (target < 64) & (source == base + target - 32)
        return jnp.where(first, -1.0, jnp.where(second, 1.0, 0.0)).astype(BF16)

    cos, sin = cosine[...], sine[...]
    for h in range(3):
        plain = ones_where((dst < HD) & (src == h * HD + dst))
        straight = dot_t(x, dot(plain, wq).astype(BF16))
        crossed = dot_t(x, dot(turned(src, dst, h * HD), wq).astype(BF16))
        q_out[pl.ds(h * SMAX, SMAX), :] = (straight * cos + crossed * sin).astype(BF16)
    straight = dot(x, wkv)
    crossed = dot(x, dot(wkv, turned(ksrc, kdst, 0)).astype(BF16))
    kv_out[...] = (straight * cos + crossed * sin).astype(BF16)


def attend_body(lane_ref, core_ref, lengths, q_ref, kv_ref, prefix_ref, w_out, mine_out, other_out):
    length, core = lengths[lane_ref[0]], core_ref[0]
    kv = kv_ref[...]
    prefix = prefix_ref[...]
    dims = (((1,), (1,)), ((), ()))
    key_at = iota((SMAX, SMAX), 1)
    keep = (key_at <= iota((SMAX, SMAX), 0)) & (key_at < length)
    heads = []
    for h in range(3):
        q = q_ref[pl.ds(h * SMAX, SMAX), :]
        far = lax.dot_general(q, prefix, dims, preferred_element_type=F32) * 0.125
        near = lax.dot_general(q, kv, dims, preferred_element_type=F32) * 0.125
        near = jnp.where(keep, near, -1e30)
        top = jnp.maximum(
            jnp.max(far, axis=-1, keepdims=True), jnp.max(near, axis=-1, keepdims=True)
        )
        far = jnp.exp(far - top)
        near = jnp.where(keep, jnp.exp(near - top), 0.0)
        total = jnp.sum(far, axis=-1, keepdims=True) + jnp.sum(near, axis=-1, keepdims=True)
        mixed = dot(far.astype(BF16), prefix) + dot(near.astype(BF16), kv)
        heads.append((mixed / total)[:, HD:].astype(BF16))
    partial = dot(jnp.concatenate(heads, axis=1), w_out[...])
    partial = partial.reshape(4, 2, ROWS, D)
    first = core == 0
    mine_out[...] = jnp.where(first, partial[:, 0], partial[:, 1])
    other_out[...] = jnp.where(first, partial[:, 1], partial[:, 0]).astype(BF16)


def add_body(a, b, out):
    out[...] = (a[...] + b[...].astype(F32)).astype(BF16)


def shuffle_matrix(transposed):
    n = 4 * REM * CHUNKS
    i = iota((n, n), 1 if transposed else 0)
    j = iota((n, n), 0 if transposed else 1)
    per = REM * CHUNKS
    same = (i % (4 * REM)) // REM == j // per
    return ones_where(same & (j % per == REM * (i // (4 * REM)) + i % REM))


def pack(main, rest, out):
    for c in range(CHUNKS):
        part = main[:, c * 128 : (c + 1) * 128].reshape(EXPERTS, MAIN, 128)
        out[:, c * MAIN : (c + 1) * MAIN, :] = part.astype(BF16)
    shuffle = shuffle_matrix(True)
    for g in range(EXPERTS // 4):
        block = rest[g * 8 : (g + 1) * 8, :]
        stacked = jnp.concatenate(
            [block[:, c * 128 : (c + 1) * 128] for c in range(CHUNKS)], axis=0
        ).astype(BF16)
        units = dot(shuffle, stacked).reshape(4, REM * CHUNKS, 128)
        out[g * 4 : (g + 1) * 4, CHUNKS * MAIN :, :] = units.astype(BF16)


def unpack(units_ref, rows_ref):
    for c in range(CHUNKS):
        part = units_ref[:, c * MAIN : (c + 1) * MAIN, :].astype(F32)
        rows_ref[0 : EXPERTS * MAIN, c * 128 : (c + 1) * 128] = part.reshape(
            EXPERTS * MAIN, 128
        ).astype(BF16)
    shuffle = shuffle_matrix(False)
    gathered = []
    for g in range(EXPERTS // 4):
        units = units_ref[g * 4 : (g + 1) * 4, CHUNKS * MAIN :, :].astype(F32)
        gathered.append(dot(shuffle, units.reshape(4 * REM * CHUNKS, 128).astype(BF16)))
    for c in range(CHUNKS):
        part = jnp.concatenate([rows[c * 8 : (c + 1) * 8] for rows in gathered], axis=0)
        rows_ref[EXPERTS * MAIN :, c * 128 : (c + 1) * 128] = part.astype(BF16)


def place_of(index):
    expert = jnp.where(index < EXPERTS * MAIN, index // MAIN, (index - EXPERTS * MAIN) // REM)
    turn = jnp.where(index < EXPERTS * MAIN, index % MAIN, MAIN + index % REM)
    return expert, turn


def picks(routes_t):
    expert = iota((EXPERTS, ROWS), 0)
    named = jnp.zeros((EXPERTS, ROWS), F32)
    for k in range(TOPK):
        named = named + ones_where(routes_t[k : k + 1, :] == expert, F32)
    named = named.astype(BF16)
    earlier = ones_where(iota((ROWS, ROWS), 0) < iota((ROWS, ROWS), 1))
    turn_of = dot(named, earlier).astype(BF16)
    total = EXPERTS * CAP
    owner, turn = place_of(iota((total, EXPERTS), 0))
    spread = ones_where(owner == iota((total, EXPERTS), 1))
    turn = turn[:, :1].astype(F32)
    return spread, (dot(spread, named) > 0.5) & (dot(spread, turn_of) == turn)


def dispatch_body(parts, states, gain, routes_t, resid_out, out):
    residual = states[...].astype(F32) + jnp.sum(parts[...].astype(F32), axis=0)
    resid_out[...] = residual
    normed = rms(residual, gain[...].astype(F32)[None]).astype(BF16)
    spread, mask = picks(routes_t)
    sent = dot(ones_where(mask), normed)
    pack(sent[: EXPERTS * MAIN], sent[EXPERTS * MAIN :], out)


def expert_body(units, gate_up_a, gate_up_b, down_a, down_b, out, rows):
    unpack(units, rows)
    x = rows[...]
    half = 256
    result = None
    for gate_up, down in ((gate_up_a, down_a), (gate_up_b, down_b)):
        pair = dot(x, gate_up[...])
        gate = pair[:, :half]
        inner = (gate * jax.nn.sigmoid(gate) * pair[:, half:]).astype(BF16)
        part = dot(inner, down[...])
        result = part if result is None else result + part
    pack(result[: EXPERTS * MAIN], result[EXPERTS * MAIN :], out)


def combine_body(lane_ref, first_ref, lengths, units, routes_t, gates_t, residual, out, rows):
    length, first = lengths[lane_ref[0]], first_ref[0]
    unpack(units, rows)
    spread, mask = picks(routes_t)
    expert = iota((EXPERTS, ROWS), 0)
    weight = jnp.zeros((EXPERTS, ROWS), F32)
    for k in range(TOPK):
        weight = jnp.where(routes_t[k : k + 1, :] == expert, gates_t[k : k + 1, :], weight)
    high = weight.astype(BF16)
    left = weight - high.astype(F32)
    middle = left.astype(BF16)
    low = (left - middle.astype(F32)).astype(BF16)
    data = rows[...]
    blend = None
    for term in (low, middle, high):
        placed = jnp.where(mask, dot(spread, term), 0.0).astype(BF16)
        part = lax.dot_general(
            placed, data, (((0,), (0,)), ((), ())), preferred_element_type=F32
        )
        blend = part if blend is None else blend + part
    live = first + iota((ROWS, 1), 0) < length
    out[...] = jnp.where(live, residual[...] + blend, 0.0).astype(BF16)


def on_device(
    states,
    gain_attn,
    gain_moe,
    w_query,
    w_keyval,
    w_out,
    prefix_cache,
    w_gate_up,
    w_down,
    routes,
    gates,
    lengths,
    group_of,
    owners,
):
    req, zs = ("x", "yh", "z1", "z0"), ("z1", "z0")
    lane = lax.axis_index(req).astype(jnp.int32)
    row = (lax.axis_index(("x", "yh")) * 8).astype(jnp.int32)[None]
    core = lax.axis_index("c").astype(jnp.int32)[None]
    first = (lax.axis_index(("l1", "l0", "c")) * ROWS).astype(jnp.int32)[None]
    lane = lane[None]
    local = states[0]
    routes_t, gates_t = routes[0].T, gates[0].T
    cosine, sine = rotary_tables()
    shape = jax.ShapeDtypeStruct
    swap = [(0, 1), (1, 0)]
    hold = lax.optimization_barrier

    with jax.named_scope("expert_swap"):
        gate_up_b = lax.ppermute(w_gate_up, "z0", swap)
        down_b = lax.ppermute(w_down, "z0", swap)
    with jax.named_scope("prefix_slices"):
        slices = lax.all_to_all(prefix_cache[0].reshape(8, 16, 128), zs, 0, 0, tiled=True)
    with jax.named_scope("norm_attn"):
        normed = call(norm_body, shape((ROWS, D), BF16), 2)(local, gain_attn)
    with jax.named_scope("prefix_copies"):
        copies = jnp.broadcast_to(slices[None], (8, 8, 16, 128))
        copies, normed = hold((copies, normed))
        held = lax.all_to_all(copies, ("x", "yh"), 0, 0, tiled=True)
    with jax.named_scope("gather_rows"):
        gathered = lax.all_gather(normed, ("l1", "l0", "c"), axis=0, tiled=True)
    with jax.named_scope("prefix_deliver"):
        held, gathered = hold((held, gathered))
        chosen = call(select_body, shape((8, PIECES, 16, 128), BF16), 4, smem=(0, 1, 2))(
            row, owners, group_of, held.reshape(64, 16, 128)
        )
        prefix = lax.all_to_all(chosen, zs, 0, 0, tiled=True).reshape(PLEN, 128)
    with jax.named_scope("project"):
        queries, keyvals = call(
            qkv_body, (shape((3 * SMAX, 128), BF16), shape((SMAX, 128), BF16)), 5
        )(gathered, w_query.T, w_keyval, cosine, sine)
    with jax.named_scope("attend"):
        prefix, queries, gate_up_b, down_b, first = hold(
            (prefix, queries, gate_up_b, down_b, first)
        )
        mine, other = call(
            attend_body,
            (shape((4, ROWS, D), F32), shape((4, ROWS, D), BF16)),
            7,
            smem=(0, 1, 2),
        )(lane, core, lengths, queries, keyvals, prefix, w_out)
    with jax.named_scope("sum_heads"):
        other = lax.ppermute(other, "c", swap)
        both = call(add_body, shape((4, ROWS, D), BF16), 2)(mine, other)
        parts = lax.all_to_all(both, ("l1", "l0"), 0, 0, tiled=True)
    with jax.named_scope("dispatch"):
        residual, outbound = call(
            dispatch_body,
            (shape((ROWS, D), F32), shape((EXPERTS, UNITS, 128), BF16)),
            4,
        )(parts, local, gain_moe, routes_t)
        inbound = lax.all_to_all(outbound, ("x", "yh", "z1"), 0, 0, tiled=True)
    with jax.named_scope("experts"):
        produced = call(
            expert_body,
            shape((EXPERTS, UNITS, 128), BF16),
            5,
            scratch=(pltpu.VMEM((EXPERTS * CAP, D), BF16),),
        )(inbound, w_gate_up[0], gate_up_b[0], w_down[0], down_b[0])
        returned = lax.all_to_all(produced, ("x", "yh", "z1"), 0, 0, tiled=True)
    with jax.named_scope("combine"):
        final = call(
            combine_body,
            shape((ROWS, D), BF16),
            7,
            smem=(0, 1, 2),
            scratch=(pltpu.VMEM((EXPERTS * CAP, D), BF16),),
        )(lane, first, lengths, returned, routes_t, gates_t, residual)
    return final[None]


def solution(mesh):
    fine = Mesh(
        mesh.devices.reshape(4, 2, 4, 2, 2, 2, 2), ("x", "yh", "z1", "z0", "l1", "l0", "c")
    )
    req, tp = ("x", "yh", "z1", "z0"), ("l1", "l0", "c")
    placed = (
        P(req, tp, None),
        P(),
        P(),
        P(None, tp),
        P(None, tp),
        P(tp, None),
        P(req, None, tp),
        P(req, None, None),
        P(req, None, None),
        P(req, tp, None),
        P(req, tp, None),
        P(),
        P(),
        P(),
    )
    return jax.shard_map(
        on_device, mesh=fine, in_specs=placed, out_specs=P(req, tp, None), check_vma=False
    )
```

```python
import math

import jax
import jax.numpy as jnp
import numpy as np
from jax import lax
from jax.experimental import pallas as pl
from jax.experimental.pallas import tpu as pltpu
from jax.sharding import Mesh, PartitionSpec as P

D = 1536
HD = 64
EXPERTS = 32
TOPK = 8
PIECES = 4
CAP = 10
MAIN = 8
REM = CAP - MAIN
ROWS = 32
CHUNKS = D // 128
UNITS = CAP * CHUNKS
PLEN = 512
SMAX = 256
F32 = jnp.float32
BF16 = jnp.bfloat16

VM = pl.BlockSpec(memory_space=pltpu.VMEM)
SM = pl.BlockSpec(memory_space=pltpu.SMEM)


def near(x):
    return pltpu.with_memory_space_constraint(x, pltpu.VMEM)


def call(body, outs, n_in, smem=(), scratch=(), far=()):
    single = not isinstance(outs, (list, tuple))
    run = pl.pallas_call(
        body,
        out_shape=outs,
        in_specs=[SM if i in smem else VM for i in range(n_in)],
        out_specs=VM if single else [VM] * len(outs),
        scratch_shapes=list(scratch),
        compiler_params=pltpu.CompilerParams(vmem_limit_bytes=24 * 2**20),
    )

    def with_near(*args):
        return run(*[x if i in smem or i in far else near(x) for i, x in enumerate(args)])

    return with_near


def dot(a, b):
    return jnp.dot(a, b, preferred_element_type=F32)


def iota(shape, dim):
    return lax.broadcasted_iota(jnp.int32, shape, dim)


def ones_where(cond, dtype=BF16):
    return jnp.where(cond, 1.0, 0.0).astype(dtype)


def rotary_tables():
    place = np.float32(PLEN) + np.arange(SMAX, dtype=np.float32)
    freq = np.exp(
        np.arange(HD // 2, dtype=np.float32) * np.float32(-2.0 * math.log(10000.0) / HD)
    ).astype(np.float32)
    angle = (place[:, None] * freq[None, :]).astype(np.float32).astype(np.float64)
    cosine, sine = np.cos(angle), np.sin(angle)
    one, zero = np.ones((SMAX, HD)), np.zeros((SMAX, HD))
    return (
        np.concatenate([cosine, cosine, one], axis=1).astype(np.float32),
        np.concatenate([sine, sine, zero], axis=1).astype(np.float32),
    )


def rms(values, gain):
    spread = lax.rsqrt(jnp.mean(values * values, axis=-1, keepdims=True) + 1e-05)
    return values * spread * gain


def norm_body(states, gain, out):
    out[...] = rms(states[...].astype(F32), gain[...].astype(F32)[None]).astype(BF16)


def select_body(base_ref, owners, group_of, held, out):
    base = base_ref[0]
    for z in range(8):
        group = group_of[base + z]
        for j in range(PIECES):
            out[z, j] = held[owners[group * PIECES + j]]


def dot_t(a, b):
    return lax.dot_general(a, b, (((1,), (1,)), ((), ())), preferred_element_type=F32)


def qkv_body(rows, w_query_t, w_keyval, cosine, sine, q_out, kv_out):
    x = rows[...]
    wq = w_query_t[...]
    wkv = w_keyval[...]
    src, dst = iota((128, 192), 1), iota((128, 192), 0)
    ksrc, kdst = iota((128, 128), 0), iota((128, 128), 1)

    def turned(source, target, base):
        first = (target < 32) & (source == base + target + 32)
        second = (target >= 32) & (target < 64) & (source == base + target - 32)
        return jnp.where(first, -1.0, jnp.where(second, 1.0, 0.0)).astype(BF16)

    cos, sin = cosine[...], sine[...]
    for h in range(3):
        plain = ones_where((dst < HD) & (src == h * HD + dst))
        straight = dot_t(x, dot(plain, wq).astype(BF16))
        crossed = dot_t(x, dot(turned(src, dst, h * HD), wq).astype(BF16))
        q_out[pl.ds(h * SMAX, SMAX), :] = (straight * cos + crossed * sin).astype(BF16)
    straight = dot(x, wkv)
    crossed = dot(x, dot(wkv, turned(ksrc, kdst, 0)).astype(BF16))
    kv_out[...] = (straight * cos + crossed * sin).astype(BF16)


def attend_body(lane_ref, core_ref, lengths, q_ref, kv_ref, prefix_ref, w_out, mine_out, other_out):
    length, core = lengths[lane_ref[0]], core_ref[0]
    kv = kv_ref[...]
    prefix = prefix_ref[...]
    dims = (((1,), (1,)), ((), ()))
    key_at = iota((SMAX, SMAX), 1)
    keep = (key_at <= iota((SMAX, SMAX), 0)) & (key_at < length)
    heads = []
    for h in range(3):
        q = q_ref[pl.ds(h * SMAX, SMAX), :]
        far = lax.dot_general(q, prefix, dims, preferred_element_type=F32) * 0.125
        near = lax.dot_general(q, kv, dims, preferred_element_type=F32) * 0.125
        near = jnp.where(keep, near, -1e30)
        top = jnp.maximum(
            jnp.max(far, axis=-1, keepdims=True), jnp.max(near, axis=-1, keepdims=True)
        )
        far = jnp.exp(far - top)
        near = jnp.where(keep, jnp.exp(near - top), 0.0)
        total = jnp.sum(far, axis=-1, keepdims=True) + jnp.sum(near, axis=-1, keepdims=True)
        mixed = dot(far.astype(BF16), prefix) + dot(near.astype(BF16), kv)
        heads.append((mixed / total)[:, HD:].astype(BF16))
    partial = dot(jnp.concatenate(heads, axis=1), w_out[...])
    partial = partial.reshape(4, 2, ROWS, D)
    first = core == 0
    mine_out[...] = jnp.where(first, partial[:, 0], partial[:, 1])
    other_out[...] = jnp.where(first, partial[:, 1], partial[:, 0]).astype(BF16)


def add_body(a, b, out):
    out[...] = (a[...] + b[...].astype(F32)).astype(BF16)


def shuffle_matrix(transposed):
    n = 4 * REM * CHUNKS
    i = iota((n, n), 1 if transposed else 0)
    j = iota((n, n), 0 if transposed else 1)
    per = REM * CHUNKS
    same = (i % (4 * REM)) // REM == j // per
    return ones_where(same & (j % per == REM * (i // (4 * REM)) + i % REM))


def pack(main, rest, out):
    for c in range(CHUNKS):
        part = main[:, c * 128 : (c + 1) * 128].reshape(EXPERTS, MAIN, 128)
        out[:, c * MAIN : (c + 1) * MAIN, :] = part.astype(BF16)
    shuffle = shuffle_matrix(True)
    for g in range(EXPERTS // 4):
        block = rest[g * 8 : (g + 1) * 8, :]
        stacked = jnp.concatenate(
            [block[:, c * 128 : (c + 1) * 128] for c in range(CHUNKS)], axis=0
        ).astype(BF16)
        units = dot(shuffle, stacked).reshape(4, REM * CHUNKS, 128)
        out[g * 4 : (g + 1) * 4, CHUNKS * MAIN :, :] = units.astype(BF16)


def unpack(units_ref, rows_ref):
    for c in range(CHUNKS):
        part = units_ref[:, c * MAIN : (c + 1) * MAIN, :].astype(F32)
        rows_ref[0 : EXPERTS * MAIN, c * 128 : (c + 1) * 128] = part.reshape(
            EXPERTS * MAIN, 128
        ).astype(BF16)
    shuffle = shuffle_matrix(False)
    gathered = []
    for g in range(EXPERTS // 4):
        units = units_ref[g * 4 : (g + 1) * 4, CHUNKS * MAIN :, :].astype(F32)
        gathered.append(dot(shuffle, units.reshape(4 * REM * CHUNKS, 128).astype(BF16)))
    for c in range(CHUNKS):
        part = jnp.concatenate([rows[c * 8 : (c + 1) * 8] for rows in gathered], axis=0)
        rows_ref[EXPERTS * MAIN :, c * 128 : (c + 1) * 128] = part.astype(BF16)


def place_of(index):
    expert = jnp.where(index < EXPERTS * MAIN, index // MAIN, (index - EXPERTS * MAIN) // REM)
    turn = jnp.where(index < EXPERTS * MAIN, index % MAIN, MAIN + index % REM)
    return expert, turn


def picks(routes_t):
    expert = iota((EXPERTS, ROWS), 0)
    named = jnp.zeros((EXPERTS, ROWS), F32)
    for k in range(TOPK):
        named = named + ones_where(routes_t[k : k + 1, :] == expert, F32)
    named = named.astype(BF16)
    earlier = ones_where(iota((ROWS, ROWS), 0) < iota((ROWS, ROWS), 1))
    turn_of = dot(named, earlier).astype(BF16)
    total = EXPERTS * CAP
    owner, turn = place_of(iota((total, EXPERTS), 0))
    spread = ones_where(owner == iota((total, EXPERTS), 1))
    turn = turn[:, :1].astype(F32)
    return spread, (dot(spread, named) > 0.5) & (dot(spread, turn_of) == turn)


def dispatch_body(parts, states, gain, routes_t, resid_out, out):
    residual = states[...].astype(F32) + jnp.sum(parts[...].astype(F32), axis=0)
    resid_out[...] = residual
    normed = rms(residual, gain[...].astype(F32)[None]).astype(BF16)
    spread, mask = picks(routes_t)
    sent = dot(ones_where(mask), normed)
    pack(sent[: EXPERTS * MAIN], sent[EXPERTS * MAIN :], out)


def expert_body(units, gate_up_a, gate_up_b, down_a, down_b, out, rows):
    unpack(units, rows)
    x = rows[...]
    half = 256
    result = None
    for gate_up, down in ((gate_up_a, down_a), (gate_up_b, down_b)):
        pair = dot(x, gate_up[...])
        gate = pair[:, :half]
        inner = (gate * jax.nn.sigmoid(gate) * pair[:, half:]).astype(BF16)
        part = dot(inner, down[...])
        result = part if result is None else result + part
    pack(result[: EXPERTS * MAIN], result[EXPERTS * MAIN :], out)


def combine_body(lane_ref, first_ref, lengths, units, routes_t, gates_t, residual, out, rows):
    length, first = lengths[lane_ref[0]], first_ref[0]
    unpack(units, rows)
    spread, mask = picks(routes_t)
    expert = iota((EXPERTS, ROWS), 0)
    weight = jnp.zeros((EXPERTS, ROWS), F32)
    for k in range(TOPK):
        weight = jnp.where(routes_t[k : k + 1, :] == expert, gates_t[k : k + 1, :], weight)
    high = weight.astype(BF16)
    left = weight - high.astype(F32)
    middle = left.astype(BF16)
    low = (left - middle.astype(F32)).astype(BF16)
    data = rows[...]
    blend = None
    for term in (low, middle, high):
        placed = jnp.where(mask, dot(spread, term), 0.0).astype(BF16)
        part = lax.dot_general(
            placed, data, (((0,), (0,)), ((), ())), preferred_element_type=F32
        )
        blend = part if blend is None else blend + part
    live = first + iota((ROWS, 1), 0) < length
    out[...] = jnp.where(live, residual[...] + blend, 0.0).astype(BF16)


def on_device(
    states,
    gain_attn,
    gain_moe,
    w_query,
    w_keyval,
    w_out,
    prefix_cache,
    w_gate_up,
    w_down,
    routes,
    gates,
    lengths,
    group_of,
    owners,
):
    req, zs = ("x", "yh", "z1", "z0"), ("z1", "z0")
    lane = lax.axis_index(req).astype(jnp.int32)
    row = (lax.axis_index(("x", "yh")) * 8).astype(jnp.int32)[None]
    core = lax.axis_index("c").astype(jnp.int32)[None]
    first = (lax.axis_index(("l1", "l0", "c")) * ROWS).astype(jnp.int32)[None]
    lane = lane[None]
    local = states[0]
    routes_t, gates_t = routes[0].T, gates[0].T
    cosine, sine = rotary_tables()
    shape = pltpu.VMEM
    swap = [(0, 1), (1, 0)]
    hold = lax.optimization_barrier

    with jax.named_scope("prefix_slices"):
        slices = lax.all_to_all(prefix_cache[0].reshape(8, 16, 128), zs, 0, 0, tiled=True)
    with jax.named_scope("norm_attn"):
        normed = call(norm_body, shape((ROWS, D), BF16), 2, far=(0, 1))(local, gain_attn)
    with jax.named_scope("prefix_copies"):
        copies = jnp.broadcast_to(slices[None], (8, 8, 16, 128))
        copies, normed, down_a = hold((copies, normed, w_down))
        held = lax.all_to_all(copies, ("x", "yh"), 0, 0, tiled=True)
    with jax.named_scope("swap_down"):
        down_b = lax.ppermute(down_a, "z0", swap)
    with jax.named_scope("gather_rows"):
        gathered = lax.all_gather(normed, ("l1", "l0", "c"), axis=0, tiled=True)
    with jax.named_scope("prefix_deliver"):
        held, gathered, down_b, first = hold((held, gathered, down_b, first))
        chosen = call(select_body, shape((8, PIECES, 16, 128), BF16), 4, smem=(0, 1, 2))(
            row, owners, group_of, held.reshape(64, 16, 128)
        )
        prefix = lax.all_to_all(chosen, zs, 0, 0, tiled=True).reshape(PLEN, 128)
    with jax.named_scope("project"):
        queries, keyvals = call(
            qkv_body,
            (shape((3 * SMAX, 128), BF16), shape((SMAX, 128), BF16)),
            5,
            far=(1, 2, 3, 4),
        )(gathered, w_query.T, w_keyval, cosine, sine)
    with jax.named_scope("swap_gate_up"):
        prefix, queries, gate_up_a = hold((prefix, queries, w_gate_up))
        gate_up_b = lax.ppermute(gate_up_a, "z0", swap)
    with jax.named_scope("attend"):
        mine, other = call(
            attend_body,
            (shape((4, ROWS, D), F32), shape((4, ROWS, D), BF16)),
            7,
            smem=(0, 1, 2),
        )(lane, core, lengths, queries, keyvals, prefix, w_out)
    with jax.named_scope("sum_heads"):
        other = lax.ppermute(other, "c", swap)
        both = call(add_body, shape((4, ROWS, D), BF16), 2)(mine, other)
        parts = lax.all_to_all(both, ("l1", "l0"), 0, 0, tiled=True)
    with jax.named_scope("dispatch"):
        residual, outbound = call(
            dispatch_body,
            (shape((ROWS, D), F32), shape((EXPERTS, UNITS, 128), BF16)),
            4,
        )(parts, local, gain_moe, routes_t)
        outbound, gate_up_b = hold((outbound, gate_up_b))
        inbound = lax.all_to_all(outbound, ("x", "yh", "z1"), 0, 0, tiled=True)
    with jax.named_scope("experts"):
        produced = call(
            expert_body,
            shape((EXPERTS, UNITS, 128), BF16),
            5,
            far=(2, 4),
            scratch=(pltpu.VMEM((EXPERTS * CAP, D), BF16),),
        )(inbound, w_gate_up[0], gate_up_b[0], w_down[0], down_b[0])
        returned = lax.all_to_all(produced, ("x", "yh", "z1"), 0, 0, tiled=True)
    with jax.named_scope("combine"):
        final = call(
            combine_body,
            jax.ShapeDtypeStruct((ROWS, D), BF16),
            7,
            smem=(0, 1, 2),
            scratch=(pltpu.VMEM((EXPERTS * CAP, D), BF16),),
        )(lane, first, lengths, returned, routes_t, gates_t, residual)
    return final[None]


def solution(mesh):
    fine = Mesh(
        mesh.devices.reshape(4, 2, 4, 2, 2, 2, 2), ("x", "yh", "z1", "z0", "l1", "l0", "c")
    )
    req, tp = ("x", "yh", "z1", "z0"), ("l1", "l0", "c")
    placed = (
        P(req, tp, None),
        P(),
        P(),
        P(None, tp),
        P(None, tp),
        P(tp, None),
        P(req, None, tp),
        P(req, None, None),
        P(req, None, None),
        P(req, tp, None),
        P(req, tp, None),
        P(),
        P(),
        P(),
    )
    return jax.shard_map(
        on_device, mesh=fine, in_specs=placed, out_specs=P(req, tp, None), check_vma=False
    )
```

```python
import math

import jax
import jax.numpy as jnp
import numpy as np
from jax import lax
from jax.experimental import pallas as pl
from jax.experimental.pallas import tpu as pltpu
from jax.sharding import Mesh, PartitionSpec as P

D = 1536
HD = 64
FF = 512
EXPERTS = 32
TOPK = 8
PIECES = 4
CAP = 10
MAIN = 8
REM = CAP - MAIN
ROWS = 32
CHUNKS = D // 128
UNITS = CAP * CHUNKS
PLEN = 512
SMAX = 256
F32 = jnp.float32
BF16 = jnp.bfloat16

VM = pl.BlockSpec(memory_space=pltpu.VMEM)
SM = pl.BlockSpec(memory_space=pltpu.SMEM)
HB = pl.BlockSpec(memory_space=pltpu.HBM)


def near(x):
    return pltpu.with_memory_space_constraint(x, pltpu.VMEM)


def call(body, outs, n_in, smem=(), scratch=(), far=()):
    single = not isinstance(outs, (list, tuple))
    run = pl.pallas_call(
        body,
        out_shape=outs,
        in_specs=[SM if i in smem else VM for i in range(n_in)],
        out_specs=VM if single else [VM] * len(outs),
        scratch_shapes=list(scratch),
        compiler_params=pltpu.CompilerParams(vmem_limit_bytes=24 * 2**20),
    )

    def with_near(*args):
        return run(*[x if i in smem or i in far else near(x) for i, x in enumerate(args)])

    return with_near


def dot(a, b):
    return jnp.dot(a, b, preferred_element_type=F32)


def iota(shape, dim):
    return lax.broadcasted_iota(jnp.int32, shape, dim)


def ones_where(cond, dtype=BF16):
    return jnp.where(cond, 1.0, 0.0).astype(dtype)


def rotary_tables():
    place = np.float32(PLEN) + np.arange(SMAX, dtype=np.float32)
    freq = np.exp(
        np.arange(HD // 2, dtype=np.float32) * np.float32(-2.0 * math.log(10000.0) / HD)
    ).astype(np.float32)
    angle = (place[:, None] * freq[None, :]).astype(np.float32).astype(np.float64)
    cosine, sine = np.cos(angle), np.sin(angle)
    one, zero = np.ones((SMAX, HD)), np.zeros((SMAX, HD))
    return (
        np.concatenate([cosine, cosine, one], axis=1).astype(np.float32),
        np.concatenate([sine, sine, zero], axis=1).astype(np.float32),
    )


def rms(values, gain):
    spread = lax.rsqrt(jnp.mean(values * values, axis=-1, keepdims=True) + 1e-05)
    return values * spread * gain


def norm_body(states, gain, out):
    out[...] = rms(states[...].astype(F32), gain[...].astype(F32)[None]).astype(BF16)


def select_body(base_ref, owners, group_of, held, out):
    base = base_ref[0]
    for z in range(8):
        group = group_of[base + z]
        for j in range(PIECES):
            out[z, j] = held[owners[group * PIECES + j]]


def dot_t(a, b):
    return lax.dot_general(a, b, (((1,), (1,)), ((), ())), preferred_element_type=F32)


def qkv_body(
    core_ref, rows, w_query_t, w_keyval, cosine, sine, gate_up, down, q_out, kv_out, packed, sems
):
    core = core_ref[0]
    depth, quarter = D // 2, FF // 4
    copies = [
        pltpu.make_async_copy(
            gate_up.at[pl.ds(core * depth, depth), :], packed.at[pl.ds(0, depth), :], sems.at[0]
        )
    ]
    for block in range(D // FF):
        copies.append(
            pltpu.make_async_copy(
                down.at[pl.ds(core * quarter, quarter), pl.ds(block * FF, FF)],
                packed.at[pl.ds(depth + block * quarter, quarter), :],
                sems.at[block + 1],
            )
        )
    for copy in copies:
        copy.start()
    x = rows[...]
    wq = w_query_t[...]
    wkv = w_keyval[...]
    src, dst = iota((128, 192), 1), iota((128, 192), 0)
    ksrc, kdst = iota((128, 128), 0), iota((128, 128), 1)

    def turned(source, target, base):
        first = (target < 32) & (source == base + target + 32)
        second = (target >= 32) & (target < 64) & (source == base + target - 32)
        return jnp.where(first, -1.0, jnp.where(second, 1.0, 0.0)).astype(BF16)

    cos, sin = cosine[...], sine[...]
    for h in range(3):
        plain = ones_where((dst < HD) & (src == h * HD + dst))
        straight = dot_t(x, dot(plain, wq).astype(BF16))
        crossed = dot_t(x, dot(turned(src, dst, h * HD), wq).astype(BF16))
        q_out[pl.ds(h * SMAX, SMAX), :] = (straight * cos + crossed * sin).astype(BF16)
    straight = dot(x, wkv)
    crossed = dot(x, dot(wkv, turned(ksrc, kdst, 0)).astype(BF16))
    kv_out[...] = (straight * cos + crossed * sin).astype(BF16)
    for copy in copies:
        copy.wait()


def attend_body(
    lane_ref, core_ref, lengths, q_ref, kv_ref, prefix_ref, w_far, mine_out, other_out, w_out, sem
):
    length, core = lengths[lane_ref[0]], core_ref[0]
    fetch = pltpu.make_async_copy(w_far, w_out, sem)
    fetch.start()
    kv = kv_ref[...]
    prefix = prefix_ref[...]
    dims = (((1,), (1,)), ((), ()))
    key_at = iota((SMAX, SMAX), 1)
    keep = (key_at <= iota((SMAX, SMAX), 0)) & (key_at < length)
    heads = []
    for h in range(3):
        q = q_ref[pl.ds(h * SMAX, SMAX), :]
        far = lax.dot_general(q, prefix, dims, preferred_element_type=F32) * 0.125
        near = lax.dot_general(q, kv, dims, preferred_element_type=F32) * 0.125
        near = jnp.where(keep, near, -1e30)
        top = jnp.maximum(
            jnp.max(far, axis=-1, keepdims=True), jnp.max(near, axis=-1, keepdims=True)
        )
        far = jnp.exp(far - top)
        near = jnp.where(keep, jnp.exp(near - top), 0.0)
        total = jnp.sum(far, axis=-1, keepdims=True) + jnp.sum(near, axis=-1, keepdims=True)
        mixed = dot(far.astype(BF16), prefix) + dot(near.astype(BF16), kv)
        heads.append((mixed / total)[:, HD:].astype(BF16))
    fetch.wait()
    partial = dot(jnp.concatenate(heads, axis=1), w_out[...])
    partial = partial.reshape(4, 2, ROWS, D)
    first = core == 0
    mine_out[...] = jnp.where(first, partial[:, 0], partial[:, 1])
    other_out[...] = jnp.where(first, partial[:, 1], partial[:, 0]).astype(BF16)


def add_body(a, b, out):
    out[...] = (a[...] + b[...].astype(F32)).astype(BF16)


def shuffle_matrix(transposed):
    n = 4 * REM * CHUNKS
    i = iota((n, n), 1 if transposed else 0)
    j = iota((n, n), 0 if transposed else 1)
    per = REM * CHUNKS
    same = (i % (4 * REM)) // REM == j // per
    return ones_where(same & (j % per == REM * (i // (4 * REM)) + i % REM))


def pack(main, rest, out):
    for c in range(CHUNKS):
        part = main[:, c * 128 : (c + 1) * 128].reshape(EXPERTS, MAIN, 128)
        out[:, c * MAIN : (c + 1) * MAIN, :] = part.astype(BF16)
    shuffle = shuffle_matrix(True)
    for g in range(EXPERTS // 4):
        block = rest[g * 8 : (g + 1) * 8, :]
        stacked = jnp.concatenate(
            [block[:, c * 128 : (c + 1) * 128] for c in range(CHUNKS)], axis=0
        ).astype(BF16)
        units = dot(shuffle, stacked).reshape(4, REM * CHUNKS, 128)
        out[g * 4 : (g + 1) * 4, CHUNKS * MAIN :, :] = units.astype(BF16)


def unpack(units_ref, rows_ref):
    for c in range(CHUNKS):
        part = units_ref[:, c * MAIN : (c + 1) * MAIN, :].astype(F32)
        rows_ref[0 : EXPERTS * MAIN, c * 128 : (c + 1) * 128] = part.reshape(
            EXPERTS * MAIN, 128
        ).astype(BF16)
    shuffle = shuffle_matrix(False)
    gathered = []
    for g in range(EXPERTS // 4):
        units = units_ref[g * 4 : (g + 1) * 4, CHUNKS * MAIN :, :].astype(F32)
        gathered.append(dot(shuffle, units.reshape(4 * REM * CHUNKS, 128).astype(BF16)))
    for c in range(CHUNKS):
        part = jnp.concatenate([rows[c * 8 : (c + 1) * 8] for rows in gathered], axis=0)
        rows_ref[EXPERTS * MAIN :, c * 128 : (c + 1) * 128] = part.astype(BF16)


def place_of(index):
    expert = jnp.where(index < EXPERTS * MAIN, index // MAIN, (index - EXPERTS * MAIN) // REM)
    turn = jnp.where(index < EXPERTS * MAIN, index % MAIN, MAIN + index % REM)
    return expert, turn


def picks(routes_t):
    expert = iota((EXPERTS, ROWS), 0)
    named = jnp.zeros((EXPERTS, ROWS), F32)
    for k in range(TOPK):
        named = named + ones_where(routes_t[k : k + 1, :] == expert, F32)
    named = named.astype(BF16)
    earlier = ones_where(iota((ROWS, ROWS), 0) < iota((ROWS, ROWS), 1))
    turn_of = dot(named, earlier).astype(BF16)
    total = EXPERTS * CAP
    owner, turn = place_of(iota((total, EXPERTS), 0))
    spread = ones_where(owner == iota((total, EXPERTS), 1))
    turn = turn[:, :1].astype(F32)
    return spread, (dot(spread, named) > 0.5) & (dot(spread, turn_of) == turn)


def dispatch_body(parts, states, gain, routes_t, resid_out, out):
    residual = states[...].astype(F32) + jnp.sum(parts[...].astype(F32), axis=0)
    resid_out[...] = residual
    normed = rms(residual, gain[...].astype(F32)[None]).astype(BF16)
    spread, mask = picks(routes_t)
    sent = dot(ones_where(mask), normed)
    pack(sent[: EXPERTS * MAIN], sent[EXPERTS * MAIN :], out)


def expert_body(core_ref, units, gate_up, down, mine, other, out, rows):
    unpack(units, rows)
    half = FF // 2
    quarter = half // 2

    def hidden(pair):
        gate = pair[:, :half]
        return (gate * jax.nn.sigmoid(gate) * pair[:, half:]).astype(BF16)

    result = dot(hidden(dot(rows[...], gate_up[...])), down[...])
    depth = D // 2
    core = core_ref[0]
    near_rows = rows[:, pl.ds(pl.multiple_of(core * depth, 128), depth)]
    far_rows = rows[:, pl.ds(pl.multiple_of((1 - core) * depth, 128), depth)]
    inner = hidden(dot(near_rows, mine[0:depth, :]) + dot(far_rows, other[0:depth, :]))
    low, high = inner[:, :quarter], inner[:, quarter:]
    own = jnp.where(core == 0, low, high)
    rest = jnp.where(core == 0, high, low)
    parts = []
    for block in range(D // FF):
        at = pl.ds(depth + block * quarter, quarter)
        parts.append(dot(own, mine[at, :]) + dot(rest, other[at, :]))
    result = result + jnp.concatenate(parts, axis=1)
    pack(result[: EXPERTS * MAIN], result[EXPERTS * MAIN :], out)


def combine_body(lane_ref, first_ref, lengths, units, routes_t, gates_t, residual, out, rows):
    length, first = lengths[lane_ref[0]], first_ref[0]
    unpack(units, rows)
    spread, mask = picks(routes_t)
    expert = iota((EXPERTS, ROWS), 0)
    weight = jnp.zeros((EXPERTS, ROWS), F32)
    for k in range(TOPK):
        weight = jnp.where(routes_t[k : k + 1, :] == expert, gates_t[k : k + 1, :], weight)
    high = weight.astype(BF16)
    left = weight - high.astype(F32)
    middle = left.astype(BF16)
    low = (left - middle.astype(F32)).astype(BF16)
    data = rows[...]
    blend = None
    for term in (low, middle, high):
        placed = jnp.where(mask, dot(spread, term), 0.0).astype(BF16)
        part = lax.dot_general(
            placed, data, (((0,), (0,)), ((), ())), preferred_element_type=F32
        )
        blend = part if blend is None else blend + part
    live = first + iota((ROWS, 1), 0) < length
    out[...] = jnp.where(live, residual[...] + blend, 0.0).astype(BF16)


def on_device(
    states,
    gain_attn,
    gain_moe,
    w_query,
    w_keyval,
    w_out,
    prefix_cache,
    w_gate_up,
    w_down,
    routes,
    gates,
    lengths,
    group_of,
    owners,
):
    req, zs = ("x", "yh", "z1", "z0"), ("z1", "z0")
    lane = lax.axis_index(req).astype(jnp.int32)
    row = (lax.axis_index(("x", "yh")) * 8).astype(jnp.int32)[None]
    core = lax.axis_index("c").astype(jnp.int32)[None]
    first = (lax.axis_index(("l1", "l0", "c")) * ROWS).astype(jnp.int32)[None]
    lane = lane[None]
    local = states[0]
    routes_t, gates_t = routes[0].T, gates[0].T
    cosine, sine = rotary_tables()
    shape = pltpu.VMEM
    swap = [(0, 1), (1, 0)]
    hold = lax.optimization_barrier

    with jax.named_scope("prefix_slices"):
        slices = prefix_cache[0].reshape(1, 8, 16, 128)
        slices = jnp.broadcast_to(slices, (8, 8, 16, 128)).reshape(64, 16, 128)
        held = lax.all_to_all(slices, req, 0, 0, tiled=True)
    with jax.named_scope("norm_attn"):
        normed = call(norm_body, shape((ROWS, D), BF16), 2, far=(0, 1))(local, gain_attn)
    with jax.named_scope("gather_rows"):
        gathered = lax.all_gather(normed, ("l1", "l0", "c"), axis=0, tiled=True)
    with jax.named_scope("prefix_deliver"):
        held, gathered, first = hold((held, gathered, first))
        chosen = call(select_body, shape((8, PIECES, 16, 128), BF16), 4, smem=(0, 1, 2))(
            row, owners, group_of, held
        )
        prefix = lax.all_to_all(chosen, zs, 0, 0, tiled=True).reshape(PLEN, 128)
    with jax.named_scope("project"):
        plain = jax.ShapeDtypeStruct
        queries, keyvals, packed = pl.pallas_call(
            qkv_body,
            out_shape=(
                plain((3 * SMAX, 128), BF16),
                plain((SMAX, 128), BF16),
                plain((D // 2 + FF // 4 * (D // FF), FF), BF16),
            ),
            in_specs=[SM] + [VM] * 5 + [HB, HB],
            out_specs=(VM, VM, HB),
            scratch_shapes=[pltpu.SemaphoreType.DMA((4,))],
            compiler_params=pltpu.CompilerParams(vmem_limit_bytes=24 * 2**20),
        )(core, near(gathered), w_query.T, w_keyval, cosine, sine, w_gate_up[0], w_down[0])
    with jax.named_scope("attend"):
        half_mine = lax.ppermute(packed, "z0", swap)
        mine, other = pl.pallas_call(
            attend_body,
            out_shape=(shape((4, ROWS, D), F32), shape((4, ROWS, D), BF16)),
            in_specs=[SM, SM, SM, VM, VM, VM, HB],
            out_specs=(VM, VM),
            scratch_shapes=[pltpu.VMEM((3 * HD, D), BF16), pltpu.SemaphoreType.DMA],
            compiler_params=pltpu.CompilerParams(vmem_limit_bytes=24 * 2**20),
        )(lane, core, lengths, queries, keyvals, near(prefix), w_out)
    with jax.named_scope("sum_heads"):
        other = lax.ppermute(other, "c", swap)
        both = call(add_body, shape((4, ROWS, D), BF16), 2)(mine, other)
        parts = lax.all_to_all(both, ("l1", "l0"), 0, 0, tiled=True)
        parts, half_mine = hold((parts, half_mine))
        half_other = lax.ppermute(half_mine, "c", swap)
    with jax.named_scope("dispatch"):
        residual, outbound = call(
            dispatch_body,
            (shape((ROWS, D), F32), shape((EXPERTS, UNITS, 128), BF16)),
            4,
        )(parts, local, gain_moe, routes_t)
        outbound, half_other = hold((outbound, half_other))
        inbound = lax.all_to_all(outbound, ("x", "yh", "z1"), 0, 0, tiled=True)
    with jax.named_scope("experts"):
        produced = call(
            expert_body,
            shape((EXPERTS, UNITS, 128), BF16),
            6,
            smem=(0,),
            far=(4, 5),
            scratch=(pltpu.VMEM((EXPERTS * CAP, D), BF16),),
        )(core, inbound, w_gate_up[0], w_down[0], half_mine, half_other)
        returned = lax.all_to_all(produced, ("x", "yh", "z1"), 0, 0, tiled=True)
    with jax.named_scope("combine"):
        final = call(
            combine_body,
            jax.ShapeDtypeStruct((ROWS, D), BF16),
            7,
            smem=(0, 1, 2),
            scratch=(pltpu.VMEM((EXPERTS * CAP, D), BF16),),
        )(lane, first, lengths, returned, routes_t, gates_t, residual)
    return final[None]


def solution(mesh):
    fine = Mesh(
        mesh.devices.reshape(4, 2, 4, 2, 2, 2, 2), ("x", "yh", "z1", "z0", "l1", "l0", "c")
    )
    req, tp = ("x", "yh", "z1", "z0"), ("l1", "l0", "c")
    placed = (
        P(req, tp, None),
        P(),
        P(),
        P(None, tp),
        P(None, tp),
        P(tp, None),
        P(req, None, tp),
        P(req, None, None),
        P(req, None, None),
        P(req, tp, None),
        P(req, tp, None),
        P(),
        P(),
        P(),
    )
    return jax.shard_map(
        on_device, mesh=fine, in_specs=placed, out_specs=P(req, tp, None), check_vma=False
    )
```

```python
import math

import jax
import jax.numpy as jnp
import numpy as np
from jax import lax
from jax.experimental import pallas as pl
from jax.experimental.pallas import tpu as pltpu
from jax.sharding import Mesh, PartitionSpec as P

D = 1536
HD = 64
FF = 512
EXPERTS = 32
TOPK = 8
PIECES = 4
CAP = 10
MAIN = 8
REM = CAP - MAIN
ROWS = 32
CHUNKS = D // 128
UNITS = CAP * CHUNKS
PLEN = 512
SMAX = 256
F32 = jnp.float32
BF16 = jnp.bfloat16

VM = pl.BlockSpec(memory_space=pltpu.VMEM)
SM = pl.BlockSpec(memory_space=pltpu.SMEM)
HB = pl.BlockSpec(memory_space=pltpu.HBM)


def near(x):
    return pltpu.with_memory_space_constraint(x, pltpu.VMEM)


def stay(x):
    return pltpu.with_memory_space_constraint(x, pltpu.HBM)


def expert_at(place):
    return place % 4 * 8 + place // 16 * 4 + place // 4 % 4


def exchange_groups():
    groups = []
    for z_set in range(2):
        for y_set in range(4):
            for core in range(2):
                group = []
                for place in range(EXPERTS):
                    yh, z1, x = place // 16, place // 4 % 4, place % 4
                    z0 = z_set ^ (z1 >> 1)
                    l = y_set ^ (2 * yh)
                    group.append(((((x * 2 + yh) * 4 + z1) * 2 + z0) * 4 + l) * 2 + core)
                groups.append(group)
    return groups


def exchange(units):
    return lax.all_to_all(
        units,
        ("x", "yh", "z1", "z0", "l1", "l0", "c"),
        0,
        0,
        axis_index_groups=exchange_groups(),
        tiled=True,
    )


def call(body, outs, n_in, smem=(), scratch=(), far=()):
    single = not isinstance(outs, (list, tuple))
    run = pl.pallas_call(
        body,
        out_shape=outs,
        in_specs=[SM if i in smem else VM for i in range(n_in)],
        out_specs=VM if single else [VM] * len(outs),
        scratch_shapes=list(scratch),
        compiler_params=pltpu.CompilerParams(vmem_limit_bytes=24 * 2**20),
    )

    def with_near(*args):
        return run(*[x if i in smem or i in far else near(x) for i, x in enumerate(args)])

    return with_near


def dot(a, b):
    return jnp.dot(a, b, preferred_element_type=F32)


def iota(shape, dim):
    return lax.broadcasted_iota(jnp.int32, shape, dim)


def ones_where(cond, dtype=BF16):
    return jnp.where(cond, 1.0, 0.0).astype(dtype)


def rotary_tables():
    place = np.float32(PLEN) + np.arange(SMAX, dtype=np.float32)
    freq = np.exp(
        np.arange(HD // 2, dtype=np.float32) * np.float32(-2.0 * math.log(10000.0) / HD)
    ).astype(np.float32)
    angle = (place[:, None] * freq[None, :]).astype(np.float32).astype(np.float64)
    cosine, sine = np.cos(angle), np.sin(angle)
    one, zero = np.ones((SMAX, HD)), np.zeros((SMAX, HD))
    return (
        np.concatenate([cosine, cosine, one], axis=1).astype(np.float32),
        np.concatenate([sine, sine, zero], axis=1).astype(np.float32),
    )


def rms(values, gain):
    spread = lax.rsqrt(jnp.mean(values * values, axis=-1, keepdims=True) + 1e-05)
    return values * spread * gain


def norm_body(states, gain, out):
    out[...] = rms(states[...].astype(F32), gain[...].astype(F32)[None]).astype(BF16)


def select_body(base_ref, owners, group_of, held, out):
    base = base_ref[0]
    for z in range(8):
        group = group_of[base + z]
        for j in range(PIECES):
            out[z, j] = held[owners[group * PIECES + j]]


def dot_t(a, b):
    return lax.dot_general(a, b, (((1,), (1,)), ((), ())), preferred_element_type=F32)


def qkv_body(
    core_ref, rows, w_query_t, w_keyval, cosine, sine, gate_up, down, q_out, kv_out, packed, sems
):
    core = core_ref[0]
    depth, quarter = D // 2, FF // 4
    copies = [
        pltpu.make_async_copy(
            gate_up.at[pl.ds(core * depth, depth), :], packed.at[pl.ds(0, depth), :], sems.at[0]
        )
    ]
    for block in range(D // FF):
        copies.append(
            pltpu.make_async_copy(
                down.at[pl.ds(core * quarter, quarter), pl.ds(block * FF, FF)],
                packed.at[pl.ds(depth + block * quarter, quarter), :],
                sems.at[block + 1],
            )
        )
    for copy in copies:
        copy.start()
    x = rows[...]
    wq = w_query_t[...]
    wkv = w_keyval[...]
    src, dst = iota((128, 192), 1), iota((128, 192), 0)
    ksrc, kdst = iota((128, 128), 0), iota((128, 128), 1)

    def turned(source, target, base):
        first = (target < 32) & (source == base + target + 32)
        second = (target >= 32) & (target < 64) & (source == base + target - 32)
        return jnp.where(first, -1.0, jnp.where(second, 1.0, 0.0)).astype(BF16)

    cos, sin = cosine[...], sine[...]
    for h in range(3):
        plain = ones_where((dst < HD) & (src == h * HD + dst))
        straight = dot_t(x, dot(plain, wq).astype(BF16))
        crossed = dot_t(x, dot(turned(src, dst, h * HD), wq).astype(BF16))
        q_out[pl.ds(h * SMAX, SMAX), :] = (straight * cos + crossed * sin).astype(BF16)
    straight = dot(x, wkv)
    crossed = dot(x, dot(wkv, turned(ksrc, kdst, 0)).astype(BF16))
    kv_out[...] = (straight * cos + crossed * sin).astype(BF16)
    for copy in copies:
        copy.wait()


def attend_body(
    lane_ref, core_ref, lengths, q_ref, kv_ref, prefix_ref, w_far, mine_out, other_out, w_out, sem
):
    length, core = lengths[lane_ref[0]], core_ref[0]
    fetch = pltpu.make_async_copy(w_far, w_out, sem)
    fetch.start()
    kv = kv_ref[...]
    prefix = prefix_ref[...]
    dims = (((1,), (1,)), ((), ()))
    key_at = iota((SMAX, SMAX), 1)
    keep = (key_at <= iota((SMAX, SMAX), 0)) & (key_at < length)
    heads = []
    for h in range(3):
        q = q_ref[pl.ds(h * SMAX, SMAX), :]
        far = lax.dot_general(q, prefix, dims, preferred_element_type=F32) * 0.125
        near = lax.dot_general(q, kv, dims, preferred_element_type=F32) * 0.125
        near = jnp.where(keep, near, -1e30)
        top = jnp.maximum(
            jnp.max(far, axis=-1, keepdims=True), jnp.max(near, axis=-1, keepdims=True)
        )
        far = jnp.exp(far - top)
        near = jnp.where(keep, jnp.exp(near - top), 0.0)
        total = jnp.sum(far, axis=-1, keepdims=True) + jnp.sum(near, axis=-1, keepdims=True)
        mixed = dot(far.astype(BF16), prefix) + dot(near.astype(BF16), kv)
        heads.append((mixed / total)[:, HD:].astype(BF16))
    fetch.wait()
    partial = dot(jnp.concatenate(heads, axis=1), w_out[...])
    partial = partial.reshape(4, 2, ROWS, D)
    first = core == 0
    mine_out[...] = jnp.where(first, partial[:, 0], partial[:, 1])
    other_out[...] = jnp.where(first, partial[:, 1], partial[:, 0]).astype(BF16)


def add_body(a, b, out):
    out[...] = (a[...] + b[...].astype(F32)).astype(BF16)


def shuffle_matrix(transposed):
    n = 4 * REM * CHUNKS
    i = iota((n, n), 1 if transposed else 0)
    j = iota((n, n), 0 if transposed else 1)
    per = REM * CHUNKS
    same = (i % (4 * REM)) // REM == j // per
    return ones_where(same & (j % per == REM * (i // (4 * REM)) + i % REM))


def pack(main, rest, out):
    for c in range(CHUNKS):
        part = main[:, c * 128 : (c + 1) * 128].reshape(EXPERTS, MAIN, 128)
        out[:, c * MAIN : (c + 1) * MAIN, :] = part.astype(BF16)
    shuffle = shuffle_matrix(True)
    for g in range(EXPERTS // 4):
        block = rest[g * 8 : (g + 1) * 8, :]
        stacked = jnp.concatenate(
            [block[:, c * 128 : (c + 1) * 128] for c in range(CHUNKS)], axis=0
        ).astype(BF16)
        units = dot(shuffle, stacked).reshape(4, REM * CHUNKS, 128)
        out[g * 4 : (g + 1) * 4, CHUNKS * MAIN :, :] = units.astype(BF16)


def unpack(units_ref, rows_ref):
    for c in range(CHUNKS):
        part = units_ref[:, c * MAIN : (c + 1) * MAIN, :].astype(F32)
        rows_ref[0 : EXPERTS * MAIN, c * 128 : (c + 1) * 128] = part.reshape(
            EXPERTS * MAIN, 128
        ).astype(BF16)
    shuffle = shuffle_matrix(False)
    gathered = []
    for g in range(EXPERTS // 4):
        units = units_ref[g * 4 : (g + 1) * 4, CHUNKS * MAIN :, :].astype(F32)
        gathered.append(dot(shuffle, units.reshape(4 * REM * CHUNKS, 128).astype(BF16)))
    for c in range(CHUNKS):
        part = jnp.concatenate([rows[c * 8 : (c + 1) * 8] for rows in gathered], axis=0)
        rows_ref[EXPERTS * MAIN :, c * 128 : (c + 1) * 128] = part.astype(BF16)


def place_of(index):
    expert = jnp.where(index < EXPERTS * MAIN, index // MAIN, (index - EXPERTS * MAIN) // REM)
    turn = jnp.where(index < EXPERTS * MAIN, index % MAIN, MAIN + index % REM)
    return expert, turn


def picks(routes_t):
    expert = expert_at(iota((EXPERTS, ROWS), 0))
    named = jnp.zeros((EXPERTS, ROWS), F32)
    for k in range(TOPK):
        named = named + ones_where(routes_t[k : k + 1, :] == expert, F32)
    named = named.astype(BF16)
    earlier = ones_where(iota((ROWS, ROWS), 0) < iota((ROWS, ROWS), 1))
    turn_of = dot(named, earlier).astype(BF16)
    total = EXPERTS * CAP
    owner, turn = place_of(iota((total, EXPERTS), 0))
    spread = ones_where(owner == iota((total, EXPERTS), 1))
    turn = turn[:, :1].astype(F32)
    return spread, (dot(spread, named) > 0.5) & (dot(spread, turn_of) == turn)


def dispatch_body(parts, states, gain, routes_t, resid_out, out):
    residual = states[...].astype(F32) + jnp.sum(parts[...].astype(F32), axis=0)
    resid_out[...] = residual
    normed = rms(residual, gain[...].astype(F32)[None]).astype(BF16)
    spread, mask = picks(routes_t)
    sent = dot(ones_where(mask), normed)
    pack(sent[: EXPERTS * MAIN], sent[EXPERTS * MAIN :], out)


def expert_body(core_ref, units, gate_up, down, mine, other, out, rows):
    unpack(units, rows)
    half = FF // 2
    quarter = half // 2

    def hidden(pair):
        gate = pair[:, :half]
        return (gate * jax.nn.sigmoid(gate) * pair[:, half:]).astype(BF16)

    result = dot(hidden(dot(rows[...], gate_up[...])), down[...])
    depth = D // 2
    core = core_ref[0]
    near_rows = rows[:, pl.ds(pl.multiple_of(core * depth, 128), depth)]
    far_rows = rows[:, pl.ds(pl.multiple_of((1 - core) * depth, 128), depth)]
    inner = hidden(dot(near_rows, mine[0:depth, :]) + dot(far_rows, other[0:depth, :]))
    low, high = inner[:, :quarter], inner[:, quarter:]
    own = jnp.where(core == 0, low, high)
    rest = jnp.where(core == 0, high, low)
    parts = []
    for block in range(D // FF):
        at = pl.ds(depth + block * quarter, quarter)
        parts.append(dot(own, mine[at, :]) + dot(rest, other[at, :]))
    result = result + jnp.concatenate(parts, axis=1)
    pack(result[: EXPERTS * MAIN], result[EXPERTS * MAIN :], out)


def combine_body(lane_ref, first_ref, lengths, units, routes_t, gates_t, residual, out, rows):
    length, first = lengths[lane_ref[0]], first_ref[0]
    unpack(units, rows)
    spread, mask = picks(routes_t)
    expert = expert_at(iota((EXPERTS, ROWS), 0))
    weight = jnp.zeros((EXPERTS, ROWS), F32)
    for k in range(TOPK):
        weight = jnp.where(routes_t[k : k + 1, :] == expert, gates_t[k : k + 1, :], weight)
    high = weight.astype(BF16)
    left = weight - high.astype(F32)
    middle = left.astype(BF16)
    low = (left - middle.astype(F32)).astype(BF16)
    data = rows[...]
    blend = None
    for term in (low, middle, high):
        placed = jnp.where(mask, dot(spread, term), 0.0).astype(BF16)
        part = lax.dot_general(
            placed, data, (((0,), (0,)), ((), ())), preferred_element_type=F32
        )
        blend = part if blend is None else blend + part
    live = first + iota((ROWS, 1), 0) < length
    out[...] = jnp.where(live, residual[...] + blend, 0.0).astype(BF16)


def on_device(
    states,
    gain_attn,
    gain_moe,
    w_query,
    w_keyval,
    w_out,
    prefix_cache,
    w_gate_up,
    w_down,
    routes,
    gates,
    lengths,
    group_of,
    owners,
):
    req, zs = ("x", "yh", "z1", "z0"), ("z1", "z0")
    lane = lax.axis_index(req).astype(jnp.int32)
    row = (lax.axis_index(("x", "yh")) * 8).astype(jnp.int32)[None]
    core = lax.axis_index("c").astype(jnp.int32)[None]
    first = (lax.axis_index(("l1", "l0", "c")) * ROWS).astype(jnp.int32)[None]
    lane = lane[None]
    local = states[0]
    routes_t, gates_t = routes[0].T, gates[0].T
    cosine, sine = rotary_tables()
    shape = pltpu.VMEM
    swap = [(0, 1), (1, 0)]
    hold = lax.optimization_barrier

    with jax.named_scope("prefix_slices"):
        slices = prefix_cache[0].reshape(1, 8, 16, 128)
        slices = jnp.broadcast_to(slices, (8, 8, 16, 128)).reshape(64, 16, 128)
        held = lax.all_to_all(slices, req, 0, 0, tiled=True)
    with jax.named_scope("norm_attn"):
        normed = call(norm_body, shape((ROWS, D), BF16), 2, far=(0, 1))(stay(local), stay(gain_attn))
    with jax.named_scope("gather_rows"):
        gathered = lax.all_gather(normed, ("l1", "l0", "c"), axis=0, tiled=True)
    with jax.named_scope("prefix_deliver"):
        held, gathered, first = hold((held, gathered, first))
        chosen = call(select_body, shape((8, PIECES, 16, 128), BF16), 4, smem=(0, 1, 2))(
            row, owners, group_of, held
        )
        prefix = lax.all_to_all(chosen, zs, 0, 0, tiled=True).reshape(PLEN, 128)
    with jax.named_scope("project"):
        plain = jax.ShapeDtypeStruct
        queries, keyvals, packed = pl.pallas_call(
            qkv_body,
            out_shape=(
                plain((3 * SMAX, 128), BF16),
                plain((SMAX, 128), BF16),
                plain((D // 2 + FF // 4 * (D // FF), FF), BF16),
            ),
            in_specs=[SM] + [VM] * 5 + [HB, HB],
            out_specs=(VM, VM, HB),
            scratch_shapes=[pltpu.SemaphoreType.DMA((4,))],
            compiler_params=pltpu.CompilerParams(vmem_limit_bytes=24 * 2**20),
        )(
            core,
            near(gathered),
            stay(w_query.T),
            stay(w_keyval),
            stay(cosine),
            stay(sine),
            w_gate_up[0],
            w_down[0],
        )
    with jax.named_scope("attend"):
        half_mine = lax.ppermute(packed, "z0", swap)
        mine, other = pl.pallas_call(
            attend_body,
            out_shape=(shape((4, ROWS, D), F32), shape((4, ROWS, D), BF16)),
            in_specs=[SM, SM, SM, VM, VM, VM, HB],
            out_specs=(VM, VM),
            scratch_shapes=[pltpu.VMEM((3 * HD, D), BF16), pltpu.SemaphoreType.DMA],
            compiler_params=pltpu.CompilerParams(vmem_limit_bytes=24 * 2**20),
        )(lane, core, lengths, queries, keyvals, near(prefix), stay(w_out))
    with jax.named_scope("sum_heads"):
        other = lax.ppermute(other, "c", swap)
        both = call(add_body, shape((4, ROWS, D), BF16), 2)(mine, other)
        parts = lax.all_to_all(both, ("l1", "l0"), 0, 0, tiled=True)
        parts, half_mine = hold((parts, half_mine))
        half_other = lax.ppermute(half_mine, "c", swap)
    with jax.named_scope("dispatch"):
        residual, outbound = call(
            dispatch_body,
            (shape((ROWS, D), F32), shape((EXPERTS, UNITS, 128), BF16)),
            4,
        )(parts, local, gain_moe, routes_t)
        outbound, half_other = hold((outbound, half_other))
        inbound = exchange(outbound)
    with jax.named_scope("experts"):
        produced = call(
            expert_body,
            shape((EXPERTS, UNITS, 128), BF16),
            6,
            smem=(0,),
            far=(4, 5),
            scratch=(pltpu.VMEM((EXPERTS * CAP, D), BF16),),
        )(core, inbound, w_gate_up[0], w_down[0], half_mine, half_other)
        returned = exchange(produced)
    with jax.named_scope("combine"):
        final = call(
            combine_body,
            jax.ShapeDtypeStruct((ROWS, D), BF16),
            7,
            smem=(0, 1, 2),
            scratch=(pltpu.VMEM((EXPERTS * CAP, D), BF16),),
        )(lane, first, lengths, returned, routes_t, gates_t, residual)
    return final[None]


def solution(mesh):
    fine = Mesh(
        mesh.devices.reshape(4, 2, 4, 2, 2, 2, 2), ("x", "yh", "z1", "z0", "l1", "l0", "c")
    )
    req, tp = ("x", "yh", "z1", "z0"), ("l1", "l0", "c")
    placed = (
        P(req, tp, None),
        P(),
        P(),
        P(None, tp),
        P(None, tp),
        P(tp, None),
        P(req, None, tp),
        P(req, None, None),
        P(req, None, None),
        P(req, tp, None),
        P(req, tp, None),
        P(),
        P(),
        P(),
    )
    return jax.shard_map(
        on_device, mesh=fine, in_specs=placed, out_specs=P(req, tp, None), check_vma=False
    )
```

```python
import math

import jax
import jax.numpy as jnp
import numpy as np
from jax import lax
from jax.experimental import pallas as pl
from jax.experimental.pallas import tpu as pltpu
from jax.sharding import Mesh, PartitionSpec as P

D = 1536
HD = 64
FF = 512
EXPERTS = 32
TOPK = 8
PIECES = 4
CAP = 10
MAIN = 8
REM = CAP - MAIN
ROWS = 32
CHUNKS = D // 128
UNITS = CAP * CHUNKS
PLEN = 512
SMAX = 256
F32 = jnp.float32
BF16 = jnp.bfloat16

VM = pl.BlockSpec(memory_space=pltpu.VMEM)
SM = pl.BlockSpec(memory_space=pltpu.SMEM)
HB = pl.BlockSpec(memory_space=pltpu.HBM)


def near(x):
    return pltpu.with_memory_space_constraint(x, pltpu.VMEM)


def stay(x):
    return pltpu.with_memory_space_constraint(x, pltpu.HBM)


def expert_at(place):
    return place % 4 * 8 + place // 16 * 4 + place // 4 % 4


def exchange_groups():
    groups = []
    for z_set in range(2):
        for y_set in range(4):
            for core in range(2):
                group = []
                for place in range(EXPERTS):
                    yh, z1, x = place // 16, place // 4 % 4, place % 4
                    z0 = z_set ^ (z1 >> 1)
                    l = y_set ^ (2 * yh)
                    group.append(((((x * 2 + yh) * 4 + z1) * 2 + z0) * 4 + l) * 2 + core)
                groups.append(group)
    return groups


def exchange(units):
    return lax.all_to_all(
        units,
        ("x", "yh", "z1", "z0", "l1", "l0", "c"),
        0,
        0,
        axis_index_groups=exchange_groups(),
        tiled=True,
    )


def call(body, outs, n_in, smem=(), scratch=(), far=()):
    single = not isinstance(outs, (list, tuple))
    run = pl.pallas_call(
        body,
        out_shape=outs,
        in_specs=[SM if i in smem else VM for i in range(n_in)],
        out_specs=VM if single else [VM] * len(outs),
        scratch_shapes=list(scratch),
        compiler_params=pltpu.CompilerParams(vmem_limit_bytes=24 * 2**20),
    )

    def with_near(*args):
        return run(*[x if i in smem or i in far else near(x) for i, x in enumerate(args)])

    return with_near


def dot(a, b):
    return jnp.dot(a, b, preferred_element_type=F32)


def iota(shape, dim):
    return lax.broadcasted_iota(jnp.int32, shape, dim)


def ones_where(cond, dtype=BF16):
    return jnp.where(cond, 1.0, 0.0).astype(dtype)


def rotary_tables():
    place = np.float32(PLEN) + np.arange(SMAX, dtype=np.float32)
    freq = np.exp(
        np.arange(HD // 2, dtype=np.float32) * np.float32(-2.0 * math.log(10000.0) / HD)
    ).astype(np.float32)
    angle = (place[:, None] * freq[None, :]).astype(np.float32).astype(np.float64)
    cosine, sine = np.cos(angle), np.sin(angle)
    one, zero = np.ones((SMAX, HD)), np.zeros((SMAX, HD))
    return (
        np.concatenate([cosine, cosine, one], axis=1).astype(np.float32),
        np.concatenate([sine, sine, zero], axis=1).astype(np.float32),
    )


def rms(values, gain):
    spread = lax.rsqrt(jnp.mean(values * values, axis=-1, keepdims=True) + 1e-05)
    return values * spread * gain


def norm_body(states, gain, piece, out, copies):
    for x in range(4):
        for z0 in range(2):
            slice_rows = piece[pl.ds((x * 2 + z0) * 16, 16), :]
            for rest in range(8):
                copies[x * 16 + rest * 2 + z0] = slice_rows
    out[...] = rms(states[...].astype(F32), gain[...].astype(F32)[None]).astype(BF16)


def select_body(base_ref, owners, group_of, held, out):
    base = base_ref[0]
    for member in range(8):
        group = group_of[base + member // 2 * 16 + member % 2]
        for j in range(PIECES):
            out[member, j] = held[owners[group * PIECES + j]]


def dot_t(a, b):
    return lax.dot_general(a, b, (((1,), (1,)), ((), ())), preferred_element_type=F32)


def qkv_body(
    core_ref, rows, w_query_t, w_keyval, cosine, sine, gate_up, down, q_out, kv_out, packed, sems
):
    core = core_ref[0]
    depth, quarter = D // 2, FF // 4
    copies = [
        pltpu.make_async_copy(
            gate_up.at[pl.ds(core * depth, depth), :], packed.at[pl.ds(0, depth), :], sems.at[0]
        )
    ]
    for block in range(D // FF):
        copies.append(
            pltpu.make_async_copy(
                down.at[pl.ds(core * quarter, quarter), pl.ds(block * FF, FF)],
                packed.at[pl.ds(depth + block * quarter, quarter), :],
                sems.at[block + 1],
            )
        )
    for copy in copies:
        copy.start()
    x = rows[...]
    wq = w_query_t[...]
    wkv = w_keyval[...]
    src, dst = iota((128, 192), 1), iota((128, 192), 0)
    ksrc, kdst = iota((128, 128), 0), iota((128, 128), 1)

    def turned(source, target, base):
        first = (target < 32) & (source == base + target + 32)
        second = (target >= 32) & (target < 64) & (source == base + target - 32)
        return jnp.where(first, -1.0, jnp.where(second, 1.0, 0.0)).astype(BF16)

    cos, sin = cosine[...], sine[...]
    for h in range(3):
        plain = ones_where((dst < HD) & (src == h * HD + dst))
        straight = dot_t(x, dot(plain, wq).astype(BF16))
        crossed = dot_t(x, dot(turned(src, dst, h * HD), wq).astype(BF16))
        q_out[pl.ds(h * SMAX, SMAX), :] = (straight * cos + crossed * sin).astype(BF16)
    straight = dot(x, wkv)
    crossed = dot(x, dot(wkv, turned(ksrc, kdst, 0)).astype(BF16))
    kv_out[...] = (straight * cos + crossed * sin).astype(BF16)
    for copy in copies:
        copy.wait()


def attend_body(
    lane_ref, core_ref, lengths, q_ref, kv_ref, prefix_ref, w_far, mine_out, other_out, w_out, sem
):
    length, core = lengths[lane_ref[0]], core_ref[0]
    fetch = pltpu.make_async_copy(w_far, w_out, sem)
    fetch.start()
    kv = kv_ref[...]
    prefix = prefix_ref[...]
    dims = (((1,), (1,)), ((), ()))
    key_at = iota((SMAX, SMAX), 1)
    keep = (key_at <= iota((SMAX, SMAX), 0)) & (key_at < length)
    heads = []
    for h in range(3):
        q = q_ref[pl.ds(h * SMAX, SMAX), :]
        far = lax.dot_general(q, prefix, dims, preferred_element_type=F32) * 0.125
        near = lax.dot_general(q, kv, dims, preferred_element_type=F32) * 0.125
        near = jnp.where(keep, near, -1e30)
        top = jnp.maximum(
            jnp.max(far, axis=-1, keepdims=True), jnp.max(near, axis=-1, keepdims=True)
        )
        far = jnp.exp(far - top)
        near = jnp.where(keep, jnp.exp(near - top), 0.0)
        total = jnp.sum(far, axis=-1, keepdims=True) + jnp.sum(near, axis=-1, keepdims=True)
        mixed = dot(far.astype(BF16), prefix) + dot(near.astype(BF16), kv)
        heads.append((mixed / total)[:, HD:].astype(BF16))
    fetch.wait()
    partial = dot(jnp.concatenate(heads, axis=1), w_out[...])
    partial = partial.reshape(4, 2, ROWS, D)
    first = core == 0
    mine_out[...] = jnp.where(first, partial[:, 0], partial[:, 1])
    other_out[...] = jnp.where(first, partial[:, 1], partial[:, 0]).astype(BF16)


def add_body(a, b, out):
    out[...] = (a[...] + b[...].astype(F32)).astype(BF16)


def shuffle_matrix(transposed):
    n = 4 * REM * CHUNKS
    i = iota((n, n), 1 if transposed else 0)
    j = iota((n, n), 0 if transposed else 1)
    per = REM * CHUNKS
    same = (i % (4 * REM)) // REM == j // per
    return ones_where(same & (j % per == REM * (i // (4 * REM)) + i % REM))


def pack(main, rest, out):
    for c in range(CHUNKS):
        part = main[:, c * 128 : (c + 1) * 128].reshape(EXPERTS, MAIN, 128)
        out[:, c * MAIN : (c + 1) * MAIN, :] = part.astype(BF16)
    shuffle = shuffle_matrix(True)
    for g in range(EXPERTS // 4):
        block = rest[g * 8 : (g + 1) * 8, :]
        stacked = jnp.concatenate(
            [block[:, c * 128 : (c + 1) * 128] for c in range(CHUNKS)], axis=0
        ).astype(BF16)
        units = dot(shuffle, stacked).reshape(4, REM * CHUNKS, 128)
        out[g * 4 : (g + 1) * 4, CHUNKS * MAIN :, :] = units.astype(BF16)


def unpack(units_ref, rows_ref):
    for c in range(CHUNKS):
        part = units_ref[:, c * MAIN : (c + 1) * MAIN, :].astype(F32)
        rows_ref[0 : EXPERTS * MAIN, c * 128 : (c + 1) * 128] = part.reshape(
            EXPERTS * MAIN, 128
        ).astype(BF16)
    shuffle = shuffle_matrix(False)
    gathered = []
    for g in range(EXPERTS // 4):
        units = units_ref[g * 4 : (g + 1) * 4, CHUNKS * MAIN :, :].astype(F32)
        gathered.append(dot(shuffle, units.reshape(4 * REM * CHUNKS, 128).astype(BF16)))
    for c in range(CHUNKS):
        part = jnp.concatenate([rows[c * 8 : (c + 1) * 8] for rows in gathered], axis=0)
        rows_ref[EXPERTS * MAIN :, c * 128 : (c + 1) * 128] = part.astype(BF16)


def place_of(index):
    expert = jnp.where(index < EXPERTS * MAIN, index // MAIN, (index - EXPERTS * MAIN) // REM)
    turn = jnp.where(index < EXPERTS * MAIN, index % MAIN, MAIN + index % REM)
    return expert, turn


def picks(routes_t):
    expert = expert_at(iota((EXPERTS, ROWS), 0))
    named = jnp.zeros((EXPERTS, ROWS), F32)
    for k in range(TOPK):
        named = named + ones_where(routes_t[k : k + 1, :] == expert, F32)
    named = named.astype(BF16)
    earlier = ones_where(iota((ROWS, ROWS), 0) < iota((ROWS, ROWS), 1))
    turn_of = dot(named, earlier).astype(BF16)
    total = EXPERTS * CAP
    owner, turn = place_of(iota((total, EXPERTS), 0))
    spread = ones_where(owner == iota((total, EXPERTS), 1))
    turn = turn[:, :1].astype(F32)
    return spread, (dot(spread, named) > 0.5) & (dot(spread, turn_of) == turn)


def dispatch_body(parts, states, gain, routes_t, resid_out, out):
    residual = states[...].astype(F32) + jnp.sum(parts[...].astype(F32), axis=0)
    resid_out[...] = residual
    normed = rms(residual, gain[...].astype(F32)[None]).astype(BF16)
    spread, mask = picks(routes_t)
    sent = dot(ones_where(mask), normed)
    pack(sent[: EXPERTS * MAIN], sent[EXPERTS * MAIN :], out)


def expert_body(core_ref, units, gate_up, down, mine, other, out, rows):
    unpack(units, rows)
    half = FF // 2
    quarter = half // 2

    def hidden(pair):
        gate = pair[:, :half]
        return (gate * jax.nn.sigmoid(gate) * pair[:, half:]).astype(BF16)

    result = dot(hidden(dot(rows[...], gate_up[...])), down[...])
    depth = D // 2
    core = core_ref[0]
    near_rows = rows[:, pl.ds(pl.multiple_of(core * depth, 128), depth)]
    far_rows = rows[:, pl.ds(pl.multiple_of((1 - core) * depth, 128), depth)]
    inner = hidden(dot(near_rows, mine[0:depth, :]) + dot(far_rows, other[0:depth, :]))
    low, high = inner[:, :quarter], inner[:, quarter:]
    own = jnp.where(core == 0, low, high)
    rest = jnp.where(core == 0, high, low)
    parts = []
    for block in range(D // FF):
        at = pl.ds(depth + block * quarter, quarter)
        parts.append(dot(own, mine[at, :]) + dot(rest, other[at, :]))
    result = result + jnp.concatenate(parts, axis=1)
    pack(result[: EXPERTS * MAIN], result[EXPERTS * MAIN :], out)


def combine_body(lane_ref, first_ref, lengths, units, routes_t, gates_t, residual, out, rows):
    length, first = lengths[lane_ref[0]], first_ref[0]
    unpack(units, rows)
    spread, mask = picks(routes_t)
    expert = expert_at(iota((EXPERTS, ROWS), 0))
    weight = jnp.zeros((EXPERTS, ROWS), F32)
    for k in range(TOPK):
        weight = jnp.where(routes_t[k : k + 1, :] == expert, gates_t[k : k + 1, :], weight)
    high = weight.astype(BF16)
    left = weight - high.astype(F32)
    middle = left.astype(BF16)
    low = (left - middle.astype(F32)).astype(BF16)
    data = rows[...]
    blend = None
    for term in (low, middle, high):
        placed = jnp.where(mask, dot(spread, term), 0.0).astype(BF16)
        part = lax.dot_general(
            placed, data, (((0,), (0,)), ((), ())), preferred_element_type=F32
        )
        blend = part if blend is None else blend + part
    live = first + iota((ROWS, 1), 0) < length
    out[...] = jnp.where(live, residual[...] + blend, 0.0).astype(BF16)


def on_device(
    states,
    gain_attn,
    gain_moe,
    w_query,
    w_keyval,
    w_out,
    prefix_cache,
    w_gate_up,
    w_down,
    routes,
    gates,
    lengths,
    group_of,
    owners,
):
    req = ("x", "yh", "z1", "z0")
    lane = lax.axis_index(req).astype(jnp.int32)
    row = (lax.axis_index(("yh", "z1")) * 2).astype(jnp.int32)[None]
    core = lax.axis_index("c").astype(jnp.int32)[None]
    first = (lax.axis_index(("l1", "l0", "c")) * ROWS).astype(jnp.int32)[None]
    lane = lane[None]
    local = states[0]
    routes_t, gates_t = routes[0].T, gates[0].T
    cosine, sine = rotary_tables()
    shape = pltpu.VMEM
    swap = [(0, 1), (1, 0)]
    hold = lax.optimization_barrier

    with jax.named_scope("norm_attn"):
        normed, copies = call(
            norm_body, (shape((ROWS, D), BF16), shape((64, 16, 128), BF16)), 3, far=(0, 1, 2)
        )(stay(local), stay(gain_attn), stay(prefix_cache[0]))
    with jax.named_scope("prefix_slices"):
        held = lax.all_to_all(copies, req, 0, 0, tiled=True)
    with jax.named_scope("gather_rows"):
        gathered = lax.all_gather(normed, ("l1", "l0", "c"), axis=0, tiled=True)
    with jax.named_scope("prefix_deliver"):
        held, gathered, first = hold((held, gathered, first))
        chosen = call(select_body, shape((8, PIECES, 16, 128), BF16), 4, smem=(0, 1, 2))(
            row, owners, group_of, held
        )
        prefix = lax.all_to_all(chosen, ("x", "z0"), 0, 0, tiled=True).reshape(PLEN, 128)
    with jax.named_scope("project"):
        plain = jax.ShapeDtypeStruct
        queries, keyvals, packed = pl.pallas_call(
            qkv_body,
            out_shape=(
                plain((3 * SMAX, 128), BF16),
                plain((SMAX, 128), BF16),
                plain((D // 2 + FF // 4 * (D // FF), FF), BF16),
            ),
            in_specs=[SM] + [VM] * 5 + [HB, HB],
            out_specs=(VM, VM, VM),
            scratch_shapes=[pltpu.SemaphoreType.DMA((4,))],
            compiler_params=pltpu.CompilerParams(vmem_limit_bytes=24 * 2**20),
        )(
            core,
            near(gathered),
            stay(w_query.T),
            stay(w_keyval),
            stay(cosine),
            stay(sine),
            stay(w_gate_up[0]),
            stay(w_down[0]),
        )
    with jax.named_scope("attend"):
        half_mine = lax.ppermute(packed, "z0", swap)
        mine, other = pl.pallas_call(
            attend_body,
            out_shape=(shape((4, ROWS, D), F32), shape((4, ROWS, D), BF16)),
            in_specs=[SM, SM, SM, VM, VM, VM, HB],
            out_specs=(VM, VM),
            scratch_shapes=[pltpu.VMEM((3 * HD, D), BF16), pltpu.SemaphoreType.DMA],
            compiler_params=pltpu.CompilerParams(vmem_limit_bytes=24 * 2**20),
        )(lane, core, lengths, queries, keyvals, near(prefix), stay(w_out))
    with jax.named_scope("sum_heads"):
        other = lax.ppermute(other, "c", swap)
        both = call(add_body, shape((4, ROWS, D), BF16), 2)(mine, other)
        parts = lax.all_to_all(both, ("l1", "l0"), 0, 0, tiled=True)
    with jax.named_scope("dispatch"):
        residual, outbound = call(
            dispatch_body,
            (shape((ROWS, D), F32), jax.ShapeDtypeStruct((EXPERTS, UNITS, 128), BF16)),
            4,
        )(parts, local, gain_moe, routes_t)
        outbound, half_mine = hold((stay(outbound), half_mine))
        half_other = lax.ppermute(half_mine, "c", swap)
        inbound = exchange(outbound)
    with jax.named_scope("experts"):
        produced = call(
            expert_body,
            shape((EXPERTS, UNITS, 128), BF16),
            6,
            smem=(0,),
            far=(4, 5),
            scratch=(pltpu.VMEM((EXPERTS * CAP, D), BF16),),
        )(core, inbound, w_gate_up[0], w_down[0], stay(half_mine), stay(half_other))
        returned = exchange(produced)
    with jax.named_scope("combine"):
        final = call(
            combine_body,
            jax.ShapeDtypeStruct((ROWS, D), BF16),
            7,
            smem=(0, 1, 2),
            scratch=(pltpu.VMEM((EXPERTS * CAP, D), BF16),),
        )(lane, first, lengths, returned, routes_t, gates_t, residual)
    return final[None]


def solution(mesh):
    fine = Mesh(
        mesh.devices.reshape(4, 2, 4, 2, 2, 2, 2), ("x", "yh", "z1", "z0", "l1", "l0", "c")
    )
    req, tp = ("x", "yh", "z1", "z0"), ("l1", "l0", "c")
    placed = (
        P(req, tp, None),
        P(),
        P(),
        P(None, tp),
        P(None, tp),
        P(tp, None),
        P(req, None, tp),
        P(req, None, None),
        P(req, None, None),
        P(req, tp, None),
        P(req, tp, None),
        P(),
        P(),
        P(),
    )
    return jax.shard_map(
        on_device, mesh=fine, in_specs=placed, out_specs=P(req, tp, None), check_vma=False
    )
```

```python
import math

import jax
import jax.numpy as jnp
import numpy as np
from jax import lax
from jax.experimental import pallas as pl
from jax.experimental.pallas import tpu as pltpu
from jax.sharding import Mesh, PartitionSpec as P

D = 1536
HD = 64
FF = 512
EXPERTS = 32
TOPK = 8
PIECES = 4
CAP = 10
MAIN = 8
REM = CAP - MAIN
ROWS = 32
CHUNKS = D // 128
UNITS = CAP * CHUNKS
PLEN = 512
SMAX = 256
F32 = jnp.float32
BF16 = jnp.bfloat16

VM = pl.BlockSpec(memory_space=pltpu.VMEM)
SM = pl.BlockSpec(memory_space=pltpu.SMEM)
HB = pl.BlockSpec(memory_space=pltpu.HBM)


def near(x):
    return pltpu.with_memory_space_constraint(x, pltpu.VMEM)


def stay(x):
    return pltpu.with_memory_space_constraint(x, pltpu.HBM)


def expert_at(place):
    return place % 4 * 8 + place // 16 * 4 + place // 4 % 4


def exchange_groups():
    groups = []
    for z_set in range(2):
        for y_set in range(4):
            for core in range(2):
                group = []
                for place in range(EXPERTS):
                    yh, z1, x = place // 16, place // 4 % 4, place % 4
                    z0 = z_set ^ (z1 >> 1)
                    l = y_set ^ (2 * yh)
                    group.append(((((x * 2 + yh) * 4 + z1) * 2 + z0) * 4 + l) * 2 + core)
                groups.append(group)
    return groups


def exchange(units):
    return lax.all_to_all(
        units,
        ("x", "yh", "z1", "z0", "l1", "l0", "c"),
        0,
        0,
        axis_index_groups=exchange_groups(),
        tiled=True,
    )


def call(body, outs, n_in, smem=(), scratch=(), far=()):
    single = not isinstance(outs, (list, tuple))
    run = pl.pallas_call(
        body,
        out_shape=outs,
        in_specs=[SM if i in smem else VM for i in range(n_in)],
        out_specs=VM if single else [VM] * len(outs),
        scratch_shapes=list(scratch),
        compiler_params=pltpu.CompilerParams(vmem_limit_bytes=24 * 2**20),
    )

    def with_near(*args):
        return run(*[x if i in smem or i in far else near(x) for i, x in enumerate(args)])

    return with_near


def dot(a, b):
    return jnp.dot(a, b, preferred_element_type=F32)


def iota(shape, dim):
    return lax.broadcasted_iota(jnp.int32, shape, dim)


def ones_where(cond, dtype=BF16):
    return jnp.where(cond, 1.0, 0.0).astype(dtype)


def rotary_tables():
    place = np.float32(PLEN) + np.arange(SMAX, dtype=np.float32)
    freq = np.exp(
        np.arange(HD // 2, dtype=np.float32) * np.float32(-2.0 * math.log(10000.0) / HD)
    ).astype(np.float32)
    angle = (place[:, None] * freq[None, :]).astype(np.float32).astype(np.float64)
    cosine, sine = np.cos(angle), np.sin(angle)
    one, zero = np.ones((SMAX, HD)), np.zeros((SMAX, HD))
    return (
        np.concatenate([cosine, cosine, one], axis=1).astype(np.float32),
        np.concatenate([sine, sine, zero], axis=1).astype(np.float32),
    )


def rms(values, gain):
    spread = lax.rsqrt(jnp.mean(values * values, axis=-1, keepdims=True) + 1e-05)
    return values * spread * gain


def norm_body(states, gain, piece, out, copies):
    for x in range(4):
        for z0 in range(2):
            slice_rows = piece[pl.ds((x * 2 + z0) * 16, 16), :]
            for rest in range(8):
                copies[x * 16 + rest * 2 + z0] = slice_rows
    out[...] = rms(states[...].astype(F32), gain[...].astype(F32)[None]).astype(BF16)


def select_body(base_ref, owners, group_of, held, out):
    base = base_ref[0]
    for member in range(8):
        group = group_of[base + member // 2 * 16 + member % 2]
        for j in range(PIECES):
            out[member, j] = held[owners[group * PIECES + j]]


def dot_t(a, b):
    return lax.dot_general(a, b, (((1,), (1,)), ((), ())), preferred_element_type=F32)


def qkv_body(
    core_ref,
    rows,
    w_query_t,
    w_keyval,
    cosine,
    sine,
    gate_up,
    down,
    q_out,
    kv_out,
    packed,
    staged,
    sems,
):
    core = core_ref[0]
    depth, quarter = D // 2, FF // 4
    copies = [
        pltpu.make_async_copy(
            gate_up.at[pl.ds(core * depth, depth), :], staged.at[pl.ds(0, depth), :], sems.at[0]
        )
    ]
    for block in range(D // FF):
        copies.append(
            pltpu.make_async_copy(
                down.at[pl.ds(core * quarter, quarter), pl.ds(block * FF, FF)],
                staged.at[pl.ds(depth + block * quarter, quarter), :],
                sems.at[block + 1],
            )
        )
    for copy in copies:
        copy.start()
    leave = pltpu.make_async_copy(staged, packed, sems.at[4])
    x = rows[...]
    wq = w_query_t[...]
    wkv = w_keyval[...]
    src, dst = iota((128, 192), 1), iota((128, 192), 0)
    ksrc, kdst = iota((128, 128), 0), iota((128, 128), 1)

    def turned(source, target, base):
        first = (target < 32) & (source == base + target + 32)
        second = (target >= 32) & (target < 64) & (source == base + target - 32)
        return jnp.where(first, -1.0, jnp.where(second, 1.0, 0.0)).astype(BF16)

    cos, sin = cosine[...], sine[...]
    for h in range(3):
        plain = ones_where((dst < HD) & (src == h * HD + dst))
        straight = dot_t(x, dot(plain, wq).astype(BF16))
        crossed = dot_t(x, dot(turned(src, dst, h * HD), wq).astype(BF16))
        q_out[pl.ds(h * SMAX, SMAX), :] = (straight * cos + crossed * sin).astype(BF16)
        if h == 0:
            for copy in copies:
                copy.wait()
            leave.start()
    straight = dot(x, wkv)
    crossed = dot(x, dot(wkv, turned(ksrc, kdst, 0)).astype(BF16))
    kv_out[...] = (straight * cos + crossed * sin).astype(BF16)
    leave.wait()


def attend_body(
    lane_ref, core_ref, lengths, q_ref, kv_ref, prefix_ref, w_far, mine_out, other_out, w_out, sem
):
    length, core = lengths[lane_ref[0]], core_ref[0]
    fetch = pltpu.make_async_copy(w_far, w_out, sem)
    fetch.start()
    kv = kv_ref[...]
    prefix = prefix_ref[...]
    dims = (((1,), (1,)), ((), ()))
    key_at = iota((SMAX, SMAX), 1)
    keep = (key_at <= iota((SMAX, SMAX), 0)) & (key_at < length)
    heads = []
    for h in range(3):
        q = q_ref[pl.ds(h * SMAX, SMAX), :]
        far = lax.dot_general(q, prefix, dims, preferred_element_type=F32) * 0.125
        near = lax.dot_general(q, kv, dims, preferred_element_type=F32) * 0.125
        near = jnp.where(keep, near, -1e30)
        top = jnp.maximum(
            jnp.max(far, axis=-1, keepdims=True), jnp.max(near, axis=-1, keepdims=True)
        )
        far = jnp.exp(far - top)
        near = jnp.where(keep, jnp.exp(near - top), 0.0)
        total = jnp.sum(far, axis=-1, keepdims=True) + jnp.sum(near, axis=-1, keepdims=True)
        mixed = dot(far.astype(BF16), prefix) + dot(near.astype(BF16), kv)
        heads.append((mixed / total)[:, HD:].astype(BF16))
    fetch.wait()
    partial = dot(jnp.concatenate(heads, axis=1), w_out[...])
    partial = partial.reshape(4, 2, ROWS, D)
    first = core == 0
    mine_out[...] = jnp.where(first, partial[:, 0], partial[:, 1])
    other_out[...] = jnp.where(first, partial[:, 1], partial[:, 0]).astype(BF16)


def add_body(a, b, out):
    out[...] = (a[...] + b[...].astype(F32)).astype(BF16)


def shuffle_matrix(transposed):
    n = 4 * REM * CHUNKS
    i = iota((n, n), 1 if transposed else 0)
    j = iota((n, n), 0 if transposed else 1)
    per = REM * CHUNKS
    same = (i % (4 * REM)) // REM == j // per
    return ones_where(same & (j % per == REM * (i // (4 * REM)) + i % REM))


def pack(main, rest, out):
    for c in range(CHUNKS):
        part = main[:, c * 128 : (c + 1) * 128].reshape(EXPERTS, MAIN, 128)
        out[:, c * MAIN : (c + 1) * MAIN, :] = part.astype(BF16)
    shuffle = shuffle_matrix(True)
    for g in range(EXPERTS // 4):
        block = rest[g * 8 : (g + 1) * 8, :]
        stacked = jnp.concatenate(
            [block[:, c * 128 : (c + 1) * 128] for c in range(CHUNKS)], axis=0
        ).astype(BF16)
        units = dot(shuffle, stacked).reshape(4, REM * CHUNKS, 128)
        out[g * 4 : (g + 1) * 4, CHUNKS * MAIN :, :] = units.astype(BF16)


def unpack(units_ref, rows_ref):
    for c in range(CHUNKS):
        part = units_ref[:, c * MAIN : (c + 1) * MAIN, :].astype(F32)
        rows_ref[0 : EXPERTS * MAIN, c * 128 : (c + 1) * 128] = part.reshape(
            EXPERTS * MAIN, 128
        ).astype(BF16)
    shuffle = shuffle_matrix(False)
    gathered = []
    for g in range(EXPERTS // 4):
        units = units_ref[g * 4 : (g + 1) * 4, CHUNKS * MAIN :, :].astype(F32)
        gathered.append(dot(shuffle, units.reshape(4 * REM * CHUNKS, 128).astype(BF16)))
    for c in range(CHUNKS):
        part = jnp.concatenate([rows[c * 8 : (c + 1) * 8] for rows in gathered], axis=0)
        rows_ref[EXPERTS * MAIN :, c * 128 : (c + 1) * 128] = part.astype(BF16)


def place_of(index):
    expert = jnp.where(index < EXPERTS * MAIN, index // MAIN, (index - EXPERTS * MAIN) // REM)
    turn = jnp.where(index < EXPERTS * MAIN, index % MAIN, MAIN + index % REM)
    return expert, turn


def picks(routes_t):
    expert = expert_at(iota((EXPERTS, ROWS), 0))
    named = jnp.zeros((EXPERTS, ROWS), F32)
    for k in range(TOPK):
        named = named + ones_where(routes_t[k : k + 1, :] == expert, F32)
    named = named.astype(BF16)
    earlier = ones_where(iota((ROWS, ROWS), 0) < iota((ROWS, ROWS), 1))
    turn_of = dot(named, earlier).astype(BF16)
    total = EXPERTS * CAP
    owner, turn = place_of(iota((total, EXPERTS), 0))
    spread = ones_where(owner == iota((total, EXPERTS), 1))
    turn = turn[:, :1].astype(F32)
    return spread, (dot(spread, named) > 0.5) & (dot(spread, turn_of) == turn)


def dispatch_body(parts, states, gain, routes_t, resid_out, out):
    residual = states[...].astype(F32) + jnp.sum(parts[...].astype(F32), axis=0)
    resid_out[...] = residual
    normed = rms(residual, gain[...].astype(F32)[None]).astype(BF16)
    spread, mask = picks(routes_t)
    sent = dot(ones_where(mask), normed)
    pack(sent[: EXPERTS * MAIN], sent[EXPERTS * MAIN :], out)


def expert_body(
    core_ref, units, gate_up, down, mine_far, other_far, out, rows, mine, other, sems
):
    fetches = [
        pltpu.make_async_copy(mine_far, mine, sems.at[0]),
        pltpu.make_async_copy(other_far, other, sems.at[1]),
    ]
    for fetch in fetches:
        fetch.start()
    unpack(units, rows)
    half = FF // 2
    quarter = half // 2

    def hidden(pair):
        gate = pair[:, :half]
        return (gate * jax.nn.sigmoid(gate) * pair[:, half:]).astype(BF16)

    result = dot(hidden(dot(rows[...], gate_up[...])), down[...])
    depth = D // 2
    core = core_ref[0]
    for fetch in fetches:
        fetch.wait()
    near_rows = rows[:, pl.ds(pl.multiple_of(core * depth, 128), depth)]
    far_rows = rows[:, pl.ds(pl.multiple_of((1 - core) * depth, 128), depth)]
    inner = hidden(dot(near_rows, mine[0:depth, :]) + dot(far_rows, other[0:depth, :]))
    low, high = inner[:, :quarter], inner[:, quarter:]
    own = jnp.where(core == 0, low, high)
    rest = jnp.where(core == 0, high, low)
    parts = []
    for block in range(D // FF):
        at = pl.ds(depth + block * quarter, quarter)
        parts.append(dot(own, mine[at, :]) + dot(rest, other[at, :]))
    result = result + jnp.concatenate(parts, axis=1)
    pack(result[: EXPERTS * MAIN], result[EXPERTS * MAIN :], out)


def combine_body(lane_ref, first_ref, lengths, units, routes_t, gates_t, residual, out, rows):
    length, first = lengths[lane_ref[0]], first_ref[0]
    unpack(units, rows)
    spread, mask = picks(routes_t)
    expert = expert_at(iota((EXPERTS, ROWS), 0))
    weight = jnp.zeros((EXPERTS, ROWS), F32)
    for k in range(TOPK):
        weight = jnp.where(routes_t[k : k + 1, :] == expert, gates_t[k : k + 1, :], weight)
    high = weight.astype(BF16)
    left = weight - high.astype(F32)
    middle = left.astype(BF16)
    low = (left - middle.astype(F32)).astype(BF16)
    data = rows[...]
    blend = None
    for term in (low, middle, high):
        placed = jnp.where(mask, dot(spread, term), 0.0).astype(BF16)
        part = lax.dot_general(
            placed, data, (((0,), (0,)), ((), ())), preferred_element_type=F32
        )
        blend = part if blend is None else blend + part
    live = first + iota((ROWS, 1), 0) < length
    out[...] = jnp.where(live, residual[...] + blend, 0.0).astype(BF16)


def on_device(
    states,
    gain_attn,
    gain_moe,
    w_query,
    w_keyval,
    w_out,
    prefix_cache,
    w_gate_up,
    w_down,
    routes,
    gates,
    lengths,
    group_of,
    owners,
):
    req = ("x", "yh", "z1", "z0")
    lane = lax.axis_index(req).astype(jnp.int32)
    row = (lax.axis_index(("yh", "z1")) * 2).astype(jnp.int32)[None]
    core = lax.axis_index("c").astype(jnp.int32)[None]
    first = (lax.axis_index(("l1", "l0", "c")) * ROWS).astype(jnp.int32)[None]
    lane = lane[None]
    local = states[0]
    routes_t, gates_t = routes[0].T, gates[0].T
    cosine, sine = rotary_tables()
    shape = pltpu.VMEM
    swap = [(0, 1), (1, 0)]
    hold = lax.optimization_barrier

    with jax.named_scope("norm_attn"):
        normed, copies = call(
            norm_body, (shape((ROWS, D), BF16), shape((64, 16, 128), BF16)), 3, far=(0, 1, 2)
        )(stay(local), stay(gain_attn), stay(prefix_cache[0]))
    with jax.named_scope("prefix_slices"):
        held = lax.all_to_all(copies, req, 0, 0, tiled=True)
    with jax.named_scope("gather_rows"):
        weights = [near(x) for x in (w_query.T, w_keyval, jnp.asarray(cosine), jnp.asarray(sine))]
        normed, *weights = hold((normed, *weights))
        gathered = lax.all_gather(normed, ("l1", "l0", "c"), axis=0, tiled=True)
    with jax.named_scope("prefix_deliver"):
        held, gathered, first = hold((held, gathered, first))
        chosen = call(select_body, shape((8, PIECES, 16, 128), BF16), 4, smem=(0, 1, 2))(
            row, owners, group_of, held
        )
        prefix = lax.all_to_all(chosen, ("x", "z0"), 0, 0, tiled=True).reshape(PLEN, 128)
    with jax.named_scope("project"):
        plain = jax.ShapeDtypeStruct
        queries, keyvals, packed = pl.pallas_call(
            qkv_body,
            out_shape=(
                plain((3 * SMAX, 128), BF16),
                plain((SMAX, 128), BF16),
                plain((D // 2 + FF // 4 * (D // FF), FF), BF16),
            ),
            in_specs=[SM] + [VM] * 5 + [HB, HB],
            out_specs=(VM, VM, HB),
            scratch_shapes=[
                pltpu.VMEM((D // 2 + FF // 4 * (D // FF), FF), BF16),
                pltpu.SemaphoreType.DMA((5,)),
            ],
            compiler_params=pltpu.CompilerParams(vmem_limit_bytes=24 * 2**20),
        )(
            core,
            near(gathered),
            *weights,
            stay(w_gate_up[0]),
            stay(w_down[0]),
        )
    with jax.named_scope("attend"):
        half_mine = lax.ppermute(packed, "z0", swap)
        mine, other = pl.pallas_call(
            attend_body,
            out_shape=(shape((4, ROWS, D), F32), shape((4, ROWS, D), BF16)),
            in_specs=[SM, SM, SM, VM, VM, VM, HB],
            out_specs=(VM, VM),
            scratch_shapes=[pltpu.VMEM((3 * HD, D), BF16), pltpu.SemaphoreType.DMA],
            compiler_params=pltpu.CompilerParams(vmem_limit_bytes=24 * 2**20),
        )(lane, core, lengths, queries, keyvals, near(prefix), stay(w_out))
    with jax.named_scope("sum_heads"):
        other = lax.ppermute(other, "c", swap)
        both = call(add_body, shape((4, ROWS, D), BF16), 2)(mine, other)
        parts = lax.all_to_all(both, ("l1", "l0"), 0, 0, tiled=True)
    with jax.named_scope("dispatch"):
        residual, outbound = call(
            dispatch_body,
            (shape((ROWS, D), F32), jax.ShapeDtypeStruct((EXPERTS, UNITS, 128), BF16)),
            4,
        )(parts, local, gain_moe, routes_t)
        outbound, half_mine = hold((stay(outbound), half_mine))
        half_other = lax.ppermute(half_mine, "c", swap)
        inbound = exchange(outbound)
    with jax.named_scope("experts"):
        packed_shape = (D // 2 + FF // 4 * (D // FF), FF)
        produced = pl.pallas_call(
            expert_body,
            out_shape=shape((EXPERTS, UNITS, 128), BF16),
            in_specs=[SM, VM, VM, VM, HB, HB],
            out_specs=VM,
            scratch_shapes=[
                pltpu.VMEM((EXPERTS * CAP, D), BF16),
                pltpu.VMEM(packed_shape, BF16),
                pltpu.VMEM(packed_shape, BF16),
                pltpu.SemaphoreType.DMA((2,)),
            ],
            compiler_params=pltpu.CompilerParams(vmem_limit_bytes=24 * 2**20),
        )(
            core,
            near(inbound),
            near(w_gate_up[0]),
            near(w_down[0]),
            stay(half_mine),
            stay(half_other),
        )
        returned = exchange(produced)
    with jax.named_scope("combine"):
        final = call(
            combine_body,
            jax.ShapeDtypeStruct((ROWS, D), BF16),
            7,
            smem=(0, 1, 2),
            scratch=(pltpu.VMEM((EXPERTS * CAP, D), BF16),),
        )(lane, first, lengths, returned, routes_t, gates_t, residual)
    return final[None]


def solution(mesh):
    fine = Mesh(
        mesh.devices.reshape(4, 2, 4, 2, 2, 2, 2), ("x", "yh", "z1", "z0", "l1", "l0", "c")
    )
    req, tp = ("x", "yh", "z1", "z0"), ("l1", "l0", "c")
    placed = (
        P(req, tp, None),
        P(),
        P(),
        P(None, tp),
        P(None, tp),
        P(tp, None),
        P(req, None, tp),
        P(req, None, None),
        P(req, None, None),
        P(req, tp, None),
        P(req, tp, None),
        P(),
        P(),
        P(),
    )
    return jax.shard_map(
        on_device, mesh=fine, in_specs=placed, out_specs=P(req, tp, None), check_vma=False
    )
```

```python
import math

import jax
import jax.numpy as jnp
import numpy as np
from jax import lax
from jax.experimental import pallas as pl
from jax.experimental.pallas import tpu as pltpu
from jax.sharding import Mesh, PartitionSpec as P

D = 1536
HD = 64
FF = 512
EXPERTS = 32
TOPK = 8
PIECES = 4
CAP = 10
MAIN = 8
REM = CAP - MAIN
ROWS = 32
CHUNKS = D // 128
UNITS = CAP * CHUNKS
PLEN = 512
SMAX = 256
F32 = jnp.float32
BF16 = jnp.bfloat16

VM = pl.BlockSpec(memory_space=pltpu.VMEM)
SM = pl.BlockSpec(memory_space=pltpu.SMEM)
HB = pl.BlockSpec(memory_space=pltpu.HBM)


def near(x):
    return pltpu.with_memory_space_constraint(x, pltpu.VMEM)


def stay(x):
    return pltpu.with_memory_space_constraint(x, pltpu.HBM)


def expert_at(place):
    return place % 4 * 8 + place // 16 * 4 + place // 4 % 4


def exchange_groups():
    groups = []
    for z_set in range(2):
        for y_set in range(4):
            for core in range(2):
                group = []
                for place in range(EXPERTS):
                    yh, z1, x = place // 16, place // 4 % 4, place % 4
                    z0 = z_set ^ (z1 >> 1)
                    l = y_set ^ (2 * yh)
                    group.append(((((x * 2 + yh) * 4 + z1) * 2 + z0) * 4 + l) * 2 + core)
                groups.append(group)
    return groups


def exchange(units):
    return lax.all_to_all(
        units,
        ("x", "yh", "z1", "z0", "l1", "l0", "c"),
        0,
        0,
        axis_index_groups=exchange_groups(),
        tiled=True,
    )


def call(body, outs, n_in, smem=(), scratch=(), far=()):
    single = not isinstance(outs, (list, tuple))
    run = pl.pallas_call(
        body,
        out_shape=outs,
        in_specs=[SM if i in smem else VM for i in range(n_in)],
        out_specs=VM if single else [VM] * len(outs),
        scratch_shapes=list(scratch),
        compiler_params=pltpu.CompilerParams(vmem_limit_bytes=24 * 2**20),
    )

    def with_near(*args):
        return run(*[x if i in smem or i in far else near(x) for i, x in enumerate(args)])

    return with_near


def dot(a, b):
    return jnp.dot(a, b, preferred_element_type=F32)


def iota(shape, dim):
    return lax.broadcasted_iota(jnp.int32, shape, dim)


def ones_where(cond, dtype=BF16):
    return jnp.where(cond, 1.0, 0.0).astype(dtype)


def rotary_tables():
    place = np.float32(PLEN) + np.arange(SMAX, dtype=np.float32)
    freq = np.exp(
        np.arange(HD // 2, dtype=np.float32) * np.float32(-2.0 * math.log(10000.0) / HD)
    ).astype(np.float32)
    angle = (place[:, None] * freq[None, :]).astype(np.float32).astype(np.float64)
    cosine, sine = np.cos(angle), np.sin(angle)
    one, zero = np.ones((SMAX, HD)), np.zeros((SMAX, HD))
    return (
        np.concatenate([cosine, cosine, one], axis=1).astype(np.float32),
        np.concatenate([sine, sine, zero], axis=1).astype(np.float32),
    )


def rms(values, gain):
    spread = lax.rsqrt(jnp.mean(values * values, axis=-1, keepdims=True) + 1e-05)
    return values * spread * gain


def norm_body(states, gain, piece, out, copies):
    for x in range(4):
        for z0 in range(2):
            slice_rows = piece[pl.ds((x * 2 + z0) * 16, 16), :]
            for rest in range(8):
                copies[x * 16 + rest * 2 + z0] = slice_rows
    out[...] = rms(states[...].astype(F32), gain[...].astype(F32)[None]).astype(BF16)


def select_body(base_ref, owners, group_of, held, out):
    base = base_ref[0]
    for member in range(8):
        group = group_of[base + member // 2 * 16 + member % 2]
        for j in range(PIECES):
            out[member, j] = held[owners[group * PIECES + j]]


def dot_t(a, b):
    return lax.dot_general(a, b, (((1,), (1,)), ((), ())), preferred_element_type=F32)


def qkv_body(
    core_ref,
    rows,
    w_query_t,
    w_keyval,
    cosine,
    sine,
    gate_up,
    down,
    q_out,
    kv_out,
    packed,
    staged,
    sems,
):
    core = core_ref[0]
    depth, quarter = D // 2, FF // 4
    copies = [
        pltpu.make_async_copy(
            gate_up.at[pl.ds(core * depth, depth), :], staged.at[pl.ds(0, depth), :], sems.at[0]
        )
    ]
    for block in range(D // FF):
        copies.append(
            pltpu.make_async_copy(
                down.at[pl.ds(core * quarter, quarter), pl.ds(block * FF, FF)],
                staged.at[pl.ds(depth + block * quarter, quarter), :],
                sems.at[block + 1],
            )
        )
    for copy in copies:
        copy.start()
    leave = pltpu.make_async_copy(staged, packed, sems.at[4])
    x = rows[...]
    wq = w_query_t[...]
    wkv = w_keyval[...]
    src, dst = iota((128, 192), 1), iota((128, 192), 0)
    ksrc, kdst = iota((128, 128), 0), iota((128, 128), 1)

    def turned(source, target, base):
        first = (target < 32) & (source == base + target + 32)
        second = (target >= 32) & (target < 64) & (source == base + target - 32)
        return jnp.where(first, -1.0, jnp.where(second, 1.0, 0.0)).astype(BF16)

    cos, sin = cosine[...], sine[...]
    for h in range(3):
        plain = ones_where((dst < HD) & (src == h * HD + dst))
        straight = dot_t(x, dot(plain, wq).astype(BF16))
        crossed = dot_t(x, dot(turned(src, dst, h * HD), wq).astype(BF16))
        q_out[pl.ds(h * SMAX, SMAX), :] = (straight * cos + crossed * sin).astype(BF16)
        if h == 0:
            for copy in copies:
                copy.wait()
            leave.start()
    straight = dot(x, wkv)
    crossed = dot(x, dot(wkv, turned(ksrc, kdst, 0)).astype(BF16))
    kv_out[...] = (straight * cos + crossed * sin).astype(BF16)
    leave.wait()


def attend_body(
    lane_ref, core_ref, lengths, q_ref, kv_ref, prefix_ref, w_far, mine_out, other_out, w_out, sem
):
    length, core = lengths[lane_ref[0]], core_ref[0]
    fetch = pltpu.make_async_copy(w_far, w_out, sem)
    fetch.start()
    kv = kv_ref[...]
    prefix = prefix_ref[...]
    dims = (((1,), (1,)), ((), ()))
    key_at = iota((SMAX, SMAX), 1)
    keep = (key_at <= iota((SMAX, SMAX), 0)) & (key_at < length)
    heads = []
    for h in range(3):
        q = q_ref[pl.ds(h * SMAX, SMAX), :]
        far = lax.dot_general(q, prefix, dims, preferred_element_type=F32) * 0.125
        near = lax.dot_general(q, kv, dims, preferred_element_type=F32) * 0.125
        near = jnp.where(keep, near, -1e30)
        top = jnp.maximum(
            jnp.max(far, axis=-1, keepdims=True), jnp.max(near, axis=-1, keepdims=True)
        )
        far = jnp.exp(far - top)
        near = jnp.where(keep, jnp.exp(near - top), 0.0)
        total = jnp.sum(far, axis=-1, keepdims=True) + jnp.sum(near, axis=-1, keepdims=True)
        mixed = dot(far.astype(BF16), prefix) + dot(near.astype(BF16), kv)
        heads.append((mixed / total)[:, HD:].astype(BF16))
    fetch.wait()
    partial = dot(jnp.concatenate(heads, axis=1), w_out[...])
    partial = partial.reshape(4, 2, ROWS, D)
    first = core == 0
    mine_out[...] = jnp.where(first, partial[:, 0], partial[:, 1])
    other_out[...] = jnp.where(first, partial[:, 1], partial[:, 0]).astype(BF16)


def add_body(a, b, out):
    out[...] = (a[...] + b[...].astype(F32)).astype(BF16)


def shuffle_matrix(transposed):
    n = 4 * REM * CHUNKS
    i = iota((n, n), 1 if transposed else 0)
    j = iota((n, n), 0 if transposed else 1)
    per = REM * CHUNKS
    same = (i % (4 * REM)) // REM == j // per
    return ones_where(same & (j % per == REM * (i // (4 * REM)) + i % REM))


def pack(main, rest, out):
    for c in range(CHUNKS):
        part = main[:, c * 128 : (c + 1) * 128].reshape(EXPERTS, MAIN, 128)
        out[:, c * MAIN : (c + 1) * MAIN, :] = part.astype(BF16)
    shuffle = shuffle_matrix(True)
    for g in range(EXPERTS // 4):
        block = rest[g * 8 : (g + 1) * 8, :]
        stacked = jnp.concatenate(
            [block[:, c * 128 : (c + 1) * 128] for c in range(CHUNKS)], axis=0
        ).astype(BF16)
        units = dot(shuffle, stacked).reshape(4, REM * CHUNKS, 128)
        out[g * 4 : (g + 1) * 4, CHUNKS * MAIN :, :] = units.astype(BF16)


def unpack(units_ref, rows_ref):
    for c in range(CHUNKS):
        part = units_ref[:, c * MAIN : (c + 1) * MAIN, :].astype(F32)
        rows_ref[0 : EXPERTS * MAIN, c * 128 : (c + 1) * 128] = part.reshape(
            EXPERTS * MAIN, 128
        ).astype(BF16)
    shuffle = shuffle_matrix(False)
    gathered = []
    for g in range(EXPERTS // 4):
        units = units_ref[g * 4 : (g + 1) * 4, CHUNKS * MAIN :, :].astype(F32)
        gathered.append(dot(shuffle, units.reshape(4 * REM * CHUNKS, 128).astype(BF16)))
    for c in range(CHUNKS):
        part = jnp.concatenate([rows[c * 8 : (c + 1) * 8] for rows in gathered], axis=0)
        rows_ref[EXPERTS * MAIN :, c * 128 : (c + 1) * 128] = part.astype(BF16)


def place_of(index):
    expert = jnp.where(index < EXPERTS * MAIN, index // MAIN, (index - EXPERTS * MAIN) // REM)
    turn = jnp.where(index < EXPERTS * MAIN, index % MAIN, MAIN + index % REM)
    return expert, turn


def picks(routes_t):
    expert = expert_at(iota((EXPERTS, ROWS), 0))
    named = jnp.zeros((EXPERTS, ROWS), F32)
    for k in range(TOPK):
        named = named + ones_where(routes_t[k : k + 1, :] == expert, F32)
    named = named.astype(BF16)
    earlier = ones_where(iota((ROWS, ROWS), 0) < iota((ROWS, ROWS), 1))
    turn_of = dot(named, earlier).astype(BF16)
    total = EXPERTS * CAP
    owner, turn = place_of(iota((total, EXPERTS), 0))
    spread = ones_where(owner == iota((total, EXPERTS), 1))
    turn = turn[:, :1].astype(F32)
    return spread, (dot(spread, named) > 0.5) & (dot(spread, turn_of) == turn)


def dispatch_body(parts, states, gain, routes_t, resid_out, out):
    residual = states[...].astype(F32) + jnp.sum(parts[...].astype(F32), axis=0)
    resid_out[...] = residual
    normed = rms(residual, gain[...].astype(F32)[None]).astype(BF16)
    spread, mask = picks(routes_t)
    sent = dot(ones_where(mask), normed)
    pack(sent[: EXPERTS * MAIN], sent[EXPERTS * MAIN :], out)


def expert_body(
    core_ref, units, gate_up, down, mine_far, other_far, out, rows, mine, other, sems
):
    fetches = [
        pltpu.make_async_copy(mine_far, mine, sems.at[0]),
        pltpu.make_async_copy(other_far, other, sems.at[1]),
    ]
    for fetch in fetches:
        fetch.start()
    unpack(units, rows)
    half = FF // 2
    quarter = half // 2

    def hidden(pair):
        gate = pair[:, :half]
        return (gate * jax.nn.sigmoid(gate) * pair[:, half:]).astype(BF16)

    result = dot(hidden(dot(rows[...], gate_up[...])), down[...])
    depth = D // 2
    core = core_ref[0]
    for fetch in fetches:
        fetch.wait()
    near_rows = rows[:, pl.ds(pl.multiple_of(core * depth, 128), depth)]
    far_rows = rows[:, pl.ds(pl.multiple_of((1 - core) * depth, 128), depth)]
    inner = hidden(dot(near_rows, mine[0:depth, :]) + dot(far_rows, other[0:depth, :]))
    low, high = inner[:, :quarter], inner[:, quarter:]
    own = jnp.where(core == 0, low, high)
    rest = jnp.where(core == 0, high, low)
    parts = []
    for block in range(D // FF):
        at = pl.ds(depth + block * quarter, quarter)
        parts.append(dot(own, mine[at, :]) + dot(rest, other[at, :]))
    result = result + jnp.concatenate(parts, axis=1)
    pack(result[: EXPERTS * MAIN], result[EXPERTS * MAIN :], out)


def combine_body(lane_ref, first_ref, lengths, units, routes_t, gates_t, residual, out, rows):
    length, first = lengths[lane_ref[0]], first_ref[0]
    unpack(units, rows)
    spread, mask = picks(routes_t)
    expert = expert_at(iota((EXPERTS, ROWS), 0))
    weight = jnp.zeros((EXPERTS, ROWS), F32)
    for k in range(TOPK):
        weight = jnp.where(routes_t[k : k + 1, :] == expert, gates_t[k : k + 1, :], weight)
    high = weight.astype(BF16)
    left = weight - high.astype(F32)
    middle = left.astype(BF16)
    low = (left - middle.astype(F32)).astype(BF16)
    placed = [jnp.where(mask, dot(spread, term), 0.0) for term in (low, middle, high)]
    placed = jnp.concatenate(placed, axis=1).T.astype(BF16)
    sums = dot(placed, rows[...])
    blend = sums[0:ROWS] + sums[ROWS : 2 * ROWS] + sums[2 * ROWS :]
    live = first + iota((ROWS, 1), 0) < length
    out[...] = jnp.where(live, residual[...] + blend, 0.0).astype(BF16)


def on_device(
    states,
    gain_attn,
    gain_moe,
    w_query,
    w_keyval,
    w_out,
    prefix_cache,
    w_gate_up,
    w_down,
    routes,
    gates,
    lengths,
    group_of,
    owners,
):
    req = ("x", "yh", "z1", "z0")
    lane = lax.axis_index(req).astype(jnp.int32)
    row = (lax.axis_index(("yh", "z1")) * 2).astype(jnp.int32)[None]
    core = lax.axis_index("c").astype(jnp.int32)[None]
    first = (lax.axis_index(("l1", "l0", "c")) * ROWS).astype(jnp.int32)[None]
    lane = lane[None]
    local = states[0]
    routes_t, gates_t = routes[0].T, gates[0].T
    cosine, sine = rotary_tables()
    shape = pltpu.VMEM
    swap = [(0, 1), (1, 0)]
    hold = lax.optimization_barrier

    with jax.named_scope("norm_attn"):
        normed, copies = call(
            norm_body, (shape((ROWS, D), BF16), shape((64, 16, 128), BF16)), 3, far=(0, 1, 2)
        )(stay(local), stay(gain_attn), stay(prefix_cache[0]))
    with jax.named_scope("prefix_slices"):
        held = lax.all_to_all(copies, req, 0, 0, tiled=True)
    with jax.named_scope("gather_rows"):
        weights = [near(x) for x in (w_query.T, w_keyval, jnp.asarray(cosine), jnp.asarray(sine))]
        normed, *weights = hold((normed, *weights))
        gathered = lax.all_gather(normed, ("l1", "l0", "c"), axis=0, tiled=True)
    with jax.named_scope("prefix_deliver"):
        held, gathered, first = hold((held, gathered, first))
        chosen = call(select_body, shape((8, PIECES, 16, 128), BF16), 4, smem=(0, 1, 2))(
            row, owners, group_of, held
        )
        prefix = lax.all_to_all(chosen, ("x", "z0"), 0, 0, tiled=True).reshape(PLEN, 128)
    with jax.named_scope("project"):
        plain = jax.ShapeDtypeStruct
        queries, keyvals, packed = pl.pallas_call(
            qkv_body,
            out_shape=(
                plain((3 * SMAX, 128), BF16),
                plain((SMAX, 128), BF16),
                plain((D // 2 + FF // 4 * (D // FF), FF), BF16),
            ),
            in_specs=[SM] + [VM] * 5 + [HB, HB],
            out_specs=(VM, VM, HB),
            scratch_shapes=[
                pltpu.VMEM((D // 2 + FF // 4 * (D // FF), FF), BF16),
                pltpu.SemaphoreType.DMA((5,)),
            ],
            compiler_params=pltpu.CompilerParams(vmem_limit_bytes=24 * 2**20),
        )(
            core,
            near(gathered),
            *weights,
            stay(w_gate_up[0]),
            stay(w_down[0]),
        )
    with jax.named_scope("attend"):
        half_mine = lax.ppermute(packed, "z0", swap)
        mine, other = pl.pallas_call(
            attend_body,
            out_shape=(shape((4, ROWS, D), F32), shape((4, ROWS, D), BF16)),
            in_specs=[SM, SM, SM, VM, VM, VM, HB],
            out_specs=(VM, VM),
            scratch_shapes=[pltpu.VMEM((3 * HD, D), BF16), pltpu.SemaphoreType.DMA],
            compiler_params=pltpu.CompilerParams(vmem_limit_bytes=24 * 2**20),
        )(lane, core, lengths, queries, keyvals, near(prefix), stay(w_out))
    with jax.named_scope("sum_heads"):
        other = lax.ppermute(other, "c", swap)
        both = call(add_body, shape((4, ROWS, D), BF16), 2)(mine, other)
        parts = lax.all_to_all(both, ("l1", "l0"), 0, 0, tiled=True)
    with jax.named_scope("dispatch"):
        residual, outbound = call(
            dispatch_body,
            (shape((ROWS, D), F32), jax.ShapeDtypeStruct((EXPERTS, UNITS, 128), BF16)),
            4,
        )(parts, local, gain_moe, routes_t)
        half_other = lax.ppermute(half_mine, "c", swap)
        inbound = exchange(outbound)
    with jax.named_scope("experts"):
        packed_shape = (D // 2 + FF // 4 * (D // FF), FF)
        produced = pl.pallas_call(
            expert_body,
            out_shape=shape((EXPERTS, UNITS, 128), BF16),
            in_specs=[SM, VM, VM, VM, HB, HB],
            out_specs=VM,
            scratch_shapes=[
                pltpu.VMEM((EXPERTS * CAP, D), BF16),
                pltpu.VMEM(packed_shape, BF16),
                pltpu.VMEM(packed_shape, BF16),
                pltpu.SemaphoreType.DMA((2,)),
            ],
            compiler_params=pltpu.CompilerParams(vmem_limit_bytes=24 * 2**20),
        )(
            core,
            near(inbound),
            near(w_gate_up[0]),
            near(w_down[0]),
            stay(half_mine),
            stay(half_other),
        )
        returned = exchange(produced)
    with jax.named_scope("combine"):
        final = call(
            combine_body,
            jax.ShapeDtypeStruct((ROWS, D), BF16),
            7,
            smem=(0, 1, 2),
            scratch=(pltpu.VMEM((EXPERTS * CAP, D), BF16),),
        )(lane, first, lengths, returned, routes_t, gates_t, residual)
    return final[None]


def solution(mesh):
    fine = Mesh(
        mesh.devices.reshape(4, 2, 4, 2, 2, 2, 2), ("x", "yh", "z1", "z0", "l1", "l0", "c")
    )
    req, tp = ("x", "yh", "z1", "z0"), ("l1", "l0", "c")
    placed = (
        P(req, tp, None),
        P(),
        P(),
        P(None, tp),
        P(None, tp),
        P(tp, None),
        P(req, None, tp),
        P(req, None, None),
        P(req, None, None),
        P(req, tp, None),
        P(req, tp, None),
        P(),
        P(),
        P(),
    )
    return jax.shard_map(
        on_device, mesh=fine, in_specs=placed, out_specs=P(req, tp, None), check_vma=False
    )
```

```python
import math

import jax
import jax.numpy as jnp
import numpy as np
from jax import lax
from jax.experimental import pallas as pl
from jax.experimental.pallas import tpu as pltpu
from jax.sharding import Mesh, PartitionSpec as P

D = 1536
HD = 64
FF = 512
EXPERTS = 32
TOPK = 8
PIECES = 4
CAP = 10
MAIN = 8
REM = CAP - MAIN
ROWS = 32
CHUNKS = D // 128
UNITS = CAP * CHUNKS
PLEN = 512
SMAX = 256
F32 = jnp.float32
BF16 = jnp.bfloat16

VM = pl.BlockSpec(memory_space=pltpu.VMEM)
SM = pl.BlockSpec(memory_space=pltpu.SMEM)
HB = pl.BlockSpec(memory_space=pltpu.HBM)


def near(x):
    return pltpu.with_memory_space_constraint(x, pltpu.VMEM)


def stay(x):
    return pltpu.with_memory_space_constraint(x, pltpu.HBM)


def expert_at(place):
    return place % 4 * 8 + place // 16 * 4 + place // 4 % 4


def exchange_groups():
    groups = []
    for z_set in range(2):
        for y_set in range(4):
            for core in range(2):
                group = []
                for place in range(EXPERTS):
                    yh, z1, x = place // 16, place // 4 % 4, place % 4
                    z0 = z_set ^ (z1 >> 1)
                    l = y_set ^ (2 * yh)
                    group.append(((((x * 2 + yh) * 4 + z1) * 2 + z0) * 4 + l) * 2 + core)
                groups.append(group)
    return groups


def exchange(units):
    return lax.all_to_all(
        units,
        ("x", "yh", "z1", "z0", "l1", "l0", "c"),
        0,
        0,
        axis_index_groups=exchange_groups(),
        tiled=True,
    )


def call(body, outs, n_in, smem=(), scratch=(), far=()):
    single = not isinstance(outs, (list, tuple))
    run = pl.pallas_call(
        body,
        out_shape=outs,
        in_specs=[SM if i in smem else VM for i in range(n_in)],
        out_specs=VM if single else [VM] * len(outs),
        scratch_shapes=list(scratch),
        compiler_params=pltpu.CompilerParams(vmem_limit_bytes=24 * 2**20),
    )

    def with_near(*args):
        return run(*[x if i in smem or i in far else near(x) for i, x in enumerate(args)])

    return with_near


def dot(a, b):
    return jnp.dot(a, b, preferred_element_type=F32)


def iota(shape, dim):
    return lax.broadcasted_iota(jnp.int32, shape, dim)


def ones_where(cond, dtype=BF16):
    return jnp.where(cond, 1.0, 0.0).astype(dtype)


def rotary_tables():
    place = np.float32(PLEN) + np.arange(SMAX, dtype=np.float32)
    freq = np.exp(
        np.arange(HD // 2, dtype=np.float32) * np.float32(-2.0 * math.log(10000.0) / HD)
    ).astype(np.float32)
    angle = (place[:, None] * freq[None, :]).astype(np.float32).astype(np.float64)
    cosine, sine = np.cos(angle), np.sin(angle)
    one, zero = np.ones((SMAX, HD)), np.zeros((SMAX, HD))
    return (
        np.concatenate([cosine, cosine, one], axis=1).astype(np.float32),
        np.concatenate([sine, sine, zero], axis=1).astype(np.float32),
    )


def rms(values, gain):
    spread = lax.rsqrt(jnp.mean(values * values, axis=-1, keepdims=True) + 1e-05)
    return values * spread * gain


def norm_body(states, gain, piece, out, copies):
    for x in range(4):
        for z0 in range(2):
            slice_rows = piece[pl.ds((x * 2 + z0) * 16, 16), :]
            for rest in range(8):
                copies[x * 16 + rest * 2 + z0] = slice_rows
    out[...] = rms(states[...].astype(F32), gain[...].astype(F32)[None]).astype(BF16)


def select_body(base_ref, owners, group_of, held, out):
    base = base_ref[0]
    for member in range(8):
        group = group_of[base + member // 2 * 16 + member % 2]
        for j in range(PIECES):
            out[member, j] = held[owners[group * PIECES + j]]


def dot_t(a, b):
    return lax.dot_general(a, b, (((1,), (1,)), ((), ())), preferred_element_type=F32)


def qkv_body(
    core_ref,
    rows,
    w_query_t,
    w_keyval,
    cosine,
    sine,
    gate_up,
    down,
    q_out,
    kv_out,
    packed,
    staged,
    sems,
):
    core = core_ref[0]
    depth, quarter = D // 2, FF // 4
    copies = [
        pltpu.make_async_copy(
            gate_up.at[pl.ds(core * depth, depth), :], staged.at[pl.ds(0, depth), :], sems.at[0]
        )
    ]
    for block in range(D // FF):
        copies.append(
            pltpu.make_async_copy(
                down.at[pl.ds(core * quarter, quarter), pl.ds(block * FF, FF)],
                staged.at[pl.ds(depth + block * quarter, quarter), :],
                sems.at[block + 1],
            )
        )
    for copy in copies:
        copy.start()
    leave = pltpu.make_async_copy(staged, packed, sems.at[4])
    x = rows[...]
    wq = w_query_t[...]
    wkv = w_keyval[...]
    src, dst = iota((128, 192), 1), iota((128, 192), 0)
    ksrc, kdst = iota((128, 128), 0), iota((128, 128), 1)

    def turned(source, target, base):
        first = (target < 32) & (source == base + target + 32)
        second = (target >= 32) & (target < 64) & (source == base + target - 32)
        return jnp.where(first, -1.0, jnp.where(second, 1.0, 0.0)).astype(BF16)

    cos, sin = cosine[...], sine[...]
    for h in range(3):
        plain = ones_where((dst < HD) & (src == h * HD + dst))
        straight = dot_t(x, dot(plain, wq).astype(BF16))
        crossed = dot_t(x, dot(turned(src, dst, h * HD), wq).astype(BF16))
        q_out[pl.ds(h * SMAX, SMAX), :] = (straight * cos + crossed * sin).astype(BF16)
        if h == 0:
            for copy in copies:
                copy.wait()
            leave.start()
    straight = dot(x, wkv)
    crossed = dot(x, dot(wkv, turned(ksrc, kdst, 0)).astype(BF16))
    kv_out[...] = (straight * cos + crossed * sin).astype(BF16)
    leave.wait()


def attend_body(
    lane_ref, core_ref, lengths, q_ref, kv_ref, prefix_ref, w_out, mine_out, other_out
):
    length, core = lengths[lane_ref[0]], core_ref[0]
    kv = kv_ref[...]
    prefix = prefix_ref[...]
    dims = (((1,), (1,)), ((), ()))
    key_at = iota((SMAX, SMAX), 1)
    keep = (key_at <= iota((SMAX, SMAX), 0)) & (key_at < length)
    heads = []
    for h in range(3):
        q = q_ref[pl.ds(h * SMAX, SMAX), :]
        far = lax.dot_general(q, prefix, dims, preferred_element_type=F32) * 0.125
        near = lax.dot_general(q, kv, dims, preferred_element_type=F32) * 0.125
        near = jnp.where(keep, near, -1e30)
        top = jnp.maximum(
            jnp.max(far, axis=-1, keepdims=True), jnp.max(near, axis=-1, keepdims=True)
        )
        far = jnp.exp(far - top)
        near = jnp.where(keep, jnp.exp(near - top), 0.0)
        total = jnp.sum(far, axis=-1, keepdims=True) + jnp.sum(near, axis=-1, keepdims=True)
        mixed = dot(far.astype(BF16), prefix) + dot(near.astype(BF16), kv)
        heads.append((mixed / total)[:, HD:].astype(BF16))
    partial = dot(jnp.concatenate(heads, axis=1), w_out[...])
    partial = partial.reshape(4, 2, ROWS, D)
    first = core == 0
    mine_out[...] = jnp.where(first, partial[:, 0], partial[:, 1])
    other_out[...] = jnp.where(first, partial[:, 1], partial[:, 0]).astype(BF16)


def add_body(a, b, out):
    out[...] = (a[...] + b[...].astype(F32)).astype(BF16)


def shuffle_matrix(transposed):
    n = 4 * REM * CHUNKS
    i = iota((n, n), 1 if transposed else 0)
    j = iota((n, n), 0 if transposed else 1)
    per = REM * CHUNKS
    same = (i % (4 * REM)) // REM == j // per
    return ones_where(same & (j % per == REM * (i // (4 * REM)) + i % REM))


def pack(main, rest, out):
    for c in range(CHUNKS):
        part = main[:, c * 128 : (c + 1) * 128].reshape(EXPERTS, MAIN, 128)
        out[:, c * MAIN : (c + 1) * MAIN, :] = part.astype(BF16)
    shuffle = shuffle_matrix(True)
    for g in range(EXPERTS // 4):
        block = rest[g * 8 : (g + 1) * 8, :]
        stacked = jnp.concatenate(
            [block[:, c * 128 : (c + 1) * 128] for c in range(CHUNKS)], axis=0
        ).astype(BF16)
        units = dot(shuffle, stacked).reshape(4, REM * CHUNKS, 128)
        out[g * 4 : (g + 1) * 4, CHUNKS * MAIN :, :] = units.astype(BF16)


def unpack(units_ref, rows_ref):
    for c in range(CHUNKS):
        part = units_ref[:, c * MAIN : (c + 1) * MAIN, :].astype(F32)
        rows_ref[0 : EXPERTS * MAIN, c * 128 : (c + 1) * 128] = part.reshape(
            EXPERTS * MAIN, 128
        ).astype(BF16)
    shuffle = shuffle_matrix(False)
    gathered = []
    for g in range(EXPERTS // 4):
        units = units_ref[g * 4 : (g + 1) * 4, CHUNKS * MAIN :, :].astype(F32)
        gathered.append(dot(shuffle, units.reshape(4 * REM * CHUNKS, 128).astype(BF16)))
    for c in range(CHUNKS):
        part = jnp.concatenate([rows[c * 8 : (c + 1) * 8] for rows in gathered], axis=0)
        rows_ref[EXPERTS * MAIN :, c * 128 : (c + 1) * 128] = part.astype(BF16)


def place_of(index):
    expert = jnp.where(index < EXPERTS * MAIN, index // MAIN, (index - EXPERTS * MAIN) // REM)
    turn = jnp.where(index < EXPERTS * MAIN, index % MAIN, MAIN + index % REM)
    return expert, turn


def picks(routes_t):
    expert = expert_at(iota((EXPERTS, ROWS), 0))
    named = jnp.zeros((EXPERTS, ROWS), F32)
    for k in range(TOPK):
        named = named + ones_where(routes_t[k : k + 1, :] == expert, F32)
    named = named.astype(BF16)
    earlier = ones_where(iota((ROWS, ROWS), 0) < iota((ROWS, ROWS), 1))
    turn_of = dot(named, earlier).astype(BF16)
    total = EXPERTS * CAP
    owner, turn = place_of(iota((total, EXPERTS), 0))
    spread = ones_where(owner == iota((total, EXPERTS), 1))
    turn = turn[:, :1].astype(F32)
    return spread, (dot(spread, named) > 0.5) & (dot(spread, turn_of) == turn)


def dispatch_body(parts, states, gain, routes_t, resid_out, out):
    residual = states[...].astype(F32) + jnp.sum(parts[...].astype(F32), axis=0)
    resid_out[...] = residual
    normed = rms(residual, gain[...].astype(F32)[None]).astype(BF16)
    spread, mask = picks(routes_t)
    sent = dot(ones_where(mask), normed)
    pack(sent[: EXPERTS * MAIN], sent[EXPERTS * MAIN :], out)


def expert_body(
    core_ref, units, gate_up, down, mine_far, other_far, out, rows, mine, other, sems
):
    fetches = [
        pltpu.make_async_copy(mine_far, mine, sems.at[0]),
        pltpu.make_async_copy(other_far, other, sems.at[1]),
    ]
    for fetch in fetches:
        fetch.start()
    unpack(units, rows)
    half = FF // 2
    quarter = half // 2

    def hidden(pair):
        gate = pair[:, :half]
        return (gate * jax.nn.sigmoid(gate) * pair[:, half:]).astype(BF16)

    result = dot(hidden(dot(rows[...], gate_up[...])), down[...])
    depth = D // 2
    core = core_ref[0]
    for fetch in fetches:
        fetch.wait()
    near_rows = rows[:, pl.ds(pl.multiple_of(core * depth, 128), depth)]
    far_rows = rows[:, pl.ds(pl.multiple_of((1 - core) * depth, 128), depth)]
    inner = hidden(dot(near_rows, mine[0:depth, :]) + dot(far_rows, other[0:depth, :]))
    low, high = inner[:, :quarter], inner[:, quarter:]
    own = jnp.where(core == 0, low, high)
    rest = jnp.where(core == 0, high, low)
    parts = []
    for block in range(D // FF):
        at = pl.ds(depth + block * quarter, quarter)
        parts.append(dot(own, mine[at, :]) + dot(rest, other[at, :]))
    result = result + jnp.concatenate(parts, axis=1)
    pack(result[: EXPERTS * MAIN], result[EXPERTS * MAIN :], out)


def combine_body(lane_ref, first_ref, lengths, units, routes_t, gates_t, residual, out, rows):
    length, first = lengths[lane_ref[0]], first_ref[0]
    unpack(units, rows)
    spread, mask = picks(routes_t)
    expert = expert_at(iota((EXPERTS, ROWS), 0))
    weight = jnp.zeros((EXPERTS, ROWS), F32)
    for k in range(TOPK):
        weight = jnp.where(routes_t[k : k + 1, :] == expert, gates_t[k : k + 1, :], weight)
    high = weight.astype(BF16)
    left = weight - high.astype(F32)
    middle = left.astype(BF16)
    low = (left - middle.astype(F32)).astype(BF16)
    placed = [jnp.where(mask, dot(spread, term), 0.0) for term in (low, middle, high)]
    placed = jnp.concatenate(placed, axis=1).T.astype(BF16)
    sums = dot(placed, rows[...])
    blend = sums[0:ROWS] + sums[ROWS : 2 * ROWS] + sums[2 * ROWS :]
    live = first + iota((ROWS, 1), 0) < length
    out[...] = jnp.where(live, residual[...] + blend, 0.0).astype(BF16)


def on_device(
    states,
    gain_attn,
    gain_moe,
    w_query,
    w_keyval,
    w_out,
    prefix_cache,
    w_gate_up,
    w_down,
    routes,
    gates,
    lengths,
    group_of,
    owners,
):
    req = ("x", "yh", "z1", "z0")
    lane = lax.axis_index(req).astype(jnp.int32)
    row = (lax.axis_index(("yh", "z1")) * 2).astype(jnp.int32)[None]
    core = lax.axis_index("c").astype(jnp.int32)[None]
    first = (lax.axis_index(("l1", "l0", "c")) * ROWS).astype(jnp.int32)[None]
    lane = lane[None]
    local = states[0]
    routes_t, gates_t = routes[0].T, gates[0].T
    cosine, sine = rotary_tables()
    shape = pltpu.VMEM
    swap = [(0, 1), (1, 0)]
    hold = lax.optimization_barrier

    with jax.named_scope("norm_attn"):
        normed, copies = call(
            norm_body, (shape((ROWS, D), BF16), shape((64, 16, 128), BF16)), 3, far=(0, 1, 2)
        )(stay(local), stay(gain_attn), stay(prefix_cache[0]))
    with jax.named_scope("prefix_slices"):
        held = lax.all_to_all(copies, req, 0, 0, tiled=True)
    with jax.named_scope("gather_rows"):
        weights = [near(x) for x in (w_query.T, w_keyval, jnp.asarray(cosine), jnp.asarray(sine))]
        normed, w_out_near, *weights = hold((normed, near(w_out), *weights))
        gathered = lax.all_gather(normed, ("l1", "l0", "c"), axis=0, tiled=True)
    with jax.named_scope("prefix_deliver"):
        held, gathered, first = hold((held, gathered, first))
        chosen = call(select_body, shape((8, PIECES, 16, 128), BF16), 4, smem=(0, 1, 2))(
            row, owners, group_of, held
        )
        prefix = lax.all_to_all(chosen, ("x", "z0"), 0, 0, tiled=True).reshape(PLEN, 128)
    with jax.named_scope("project"):
        plain = jax.ShapeDtypeStruct
        queries, keyvals, packed = pl.pallas_call(
            qkv_body,
            out_shape=(
                plain((3 * SMAX, 128), BF16),
                plain((SMAX, 128), BF16),
                plain((D // 2 + FF // 4 * (D // FF), FF), BF16),
            ),
            in_specs=[SM] + [VM] * 5 + [HB, HB],
            out_specs=(VM, VM, HB),
            scratch_shapes=[
                pltpu.VMEM((D // 2 + FF // 4 * (D // FF), FF), BF16),
                pltpu.SemaphoreType.DMA((5,)),
            ],
            compiler_params=pltpu.CompilerParams(vmem_limit_bytes=24 * 2**20),
        )(
            core,
            near(gathered),
            *weights,
            stay(w_gate_up[0]),
            stay(w_down[0]),
        )
    with jax.named_scope("attend"):
        half_mine = lax.ppermute(packed, "z0", swap)
        mine, other = pl.pallas_call(
            attend_body,
            out_shape=(shape((4, ROWS, D), F32), shape((4, ROWS, D), BF16)),
            in_specs=[SM, SM, SM, VM, VM, VM, VM],
            out_specs=(VM, VM),
            compiler_params=pltpu.CompilerParams(vmem_limit_bytes=24 * 2**20),
        )(lane, core, lengths, queries, keyvals, near(prefix), w_out_near)
    with jax.named_scope("sum_heads"):
        other = lax.ppermute(other, "c", swap)
        both = call(add_body, shape((4, ROWS, D), BF16), 2)(mine, other)
        parts = lax.all_to_all(both, ("l1", "l0"), 0, 0, tiled=True)
    with jax.named_scope("dispatch"):
        residual, outbound = call(
            dispatch_body,
            (shape((ROWS, D), F32), jax.ShapeDtypeStruct((EXPERTS, UNITS, 128), BF16)),
            4,
        )(parts, local, gain_moe, routes_t)
        half_other = lax.ppermute(half_mine, "c", swap)
        inbound = exchange(outbound)
    with jax.named_scope("experts"):
        packed_shape = (D // 2 + FF // 4 * (D // FF), FF)
        produced = pl.pallas_call(
            expert_body,
            out_shape=shape((EXPERTS, UNITS, 128), BF16),
            in_specs=[SM, VM, VM, VM, HB, HB],
            out_specs=VM,
            scratch_shapes=[
                pltpu.VMEM((EXPERTS * CAP, D), BF16),
                pltpu.VMEM(packed_shape, BF16),
                pltpu.VMEM(packed_shape, BF16),
                pltpu.SemaphoreType.DMA((2,)),
            ],
            compiler_params=pltpu.CompilerParams(vmem_limit_bytes=24 * 2**20),
        )(
            core,
            near(inbound),
            near(w_gate_up[0]),
            near(w_down[0]),
            stay(half_mine),
            stay(half_other),
        )
        returned = exchange(produced)
    with jax.named_scope("combine"):
        final = call(
            combine_body,
            jax.ShapeDtypeStruct((ROWS, D), BF16),
            7,
            smem=(0, 1, 2),
            scratch=(pltpu.VMEM((EXPERTS * CAP, D), BF16),),
        )(lane, first, lengths, returned, routes_t, gates_t, residual)
    return final[None]


def solution(mesh):
    fine = Mesh(
        mesh.devices.reshape(4, 2, 4, 2, 2, 2, 2), ("x", "yh", "z1", "z0", "l1", "l0", "c")
    )
    req, tp = ("x", "yh", "z1", "z0"), ("l1", "l0", "c")
    placed = (
        P(req, tp, None),
        P(),
        P(),
        P(None, tp),
        P(None, tp),
        P(tp, None),
        P(req, None, tp),
        P(req, None, None),
        P(req, None, None),
        P(req, tp, None),
        P(req, tp, None),
        P(),
        P(),
        P(),
    )
    return jax.shard_map(
        on_device, mesh=fine, in_specs=placed, out_specs=P(req, tp, None), check_vma=False
    )
```

```python
import math

import jax
import jax.numpy as jnp
import numpy as np
from jax import lax
from jax.experimental import pallas as pl
from jax.experimental.pallas import tpu as pltpu
from jax.sharding import Mesh, PartitionSpec as P

D = 1536
HD = 64
FF = 512
EXPERTS = 32
TOPK = 8
PIECES = 4
CAP = 10
MAIN = 8
REM = CAP - MAIN
ROWS = 32
CHUNKS = D // 128
UNITS = CAP * CHUNKS
PLEN = 512
SMAX = 256
F32 = jnp.float32
BF16 = jnp.bfloat16

VM = pl.BlockSpec(memory_space=pltpu.VMEM)
SM = pl.BlockSpec(memory_space=pltpu.SMEM)
HB = pl.BlockSpec(memory_space=pltpu.HBM)


def near(x):
    return pltpu.with_memory_space_constraint(x, pltpu.VMEM)


def stay(x):
    return pltpu.with_memory_space_constraint(x, pltpu.HBM)


def expert_at(place):
    return place % 4 * 8 + place // 16 * 4 + place // 4 % 4


def exchange_groups():
    groups = []
    for z_set in range(2):
        for y_set in range(4):
            for core in range(2):
                group = []
                for place in range(EXPERTS):
                    yh, z1, x = place // 16, place // 4 % 4, place % 4
                    z0 = z_set ^ (z1 >> 1)
                    l = y_set ^ (2 * yh)
                    group.append(((((x * 2 + yh) * 4 + z1) * 2 + z0) * 4 + l) * 2 + core)
                groups.append(group)
    return groups


def exchange(units):
    return lax.all_to_all(
        units,
        ("x", "yh", "z1", "z0", "l1", "l0", "c"),
        0,
        0,
        axis_index_groups=exchange_groups(),
        tiled=True,
    )


def call(body, outs, n_in, smem=(), scratch=(), far=()):
    single = not isinstance(outs, (list, tuple))
    run = pl.pallas_call(
        body,
        out_shape=outs,
        in_specs=[SM if i in smem else VM for i in range(n_in)],
        out_specs=VM if single else [VM] * len(outs),
        scratch_shapes=list(scratch),
        compiler_params=pltpu.CompilerParams(vmem_limit_bytes=24 * 2**20),
    )

    def with_near(*args):
        return run(*[x if i in smem or i in far else near(x) for i, x in enumerate(args)])

    return with_near


def dot(a, b):
    return jnp.dot(a, b, preferred_element_type=F32)


def iota(shape, dim):
    return lax.broadcasted_iota(jnp.int32, shape, dim)


def ones_where(cond, dtype=BF16):
    return jnp.where(cond, 1.0, 0.0).astype(dtype)


def rotary_tables():
    place = np.float32(PLEN) + np.arange(SMAX, dtype=np.float32)
    freq = np.exp(
        np.arange(HD // 2, dtype=np.float32) * np.float32(-2.0 * math.log(10000.0) / HD)
    ).astype(np.float32)
    angle = (place[:, None] * freq[None, :]).astype(np.float32).astype(np.float64)
    cosine, sine = np.cos(angle), np.sin(angle)
    one, zero = np.ones((SMAX, HD)), np.zeros((SMAX, HD))
    return (
        np.concatenate([cosine, cosine, one], axis=1).astype(np.float32),
        np.concatenate([sine, sine, zero], axis=1).astype(np.float32),
    )


def rms(values, gain):
    spread = lax.rsqrt(jnp.mean(values * values, axis=-1, keepdims=True) + 1e-05)
    return values * spread * gain


def norm_body(states, gain, piece, out, copies):
    for x in range(4):
        for z0 in range(2):
            slice_rows = piece[pl.ds((x * 2 + z0) * 16, 16), :]
            for rest in range(8):
                copies[x * 16 + rest * 2 + z0] = slice_rows
    out[...] = rms(states[...].astype(F32), gain[...].astype(F32)[None]).astype(BF16)


def select_body(base_ref, owners, group_of, held, out):
    base = base_ref[0]
    for member in range(8):
        group = group_of[base + member // 2 * 16 + member % 2]
        for j in range(PIECES):
            out[member, j] = held[owners[group * PIECES + j]]


def dot_t(a, b):
    return lax.dot_general(a, b, (((1,), (1,)), ((), ())), preferred_element_type=F32)


def qkv_body(
    core_ref,
    rows,
    w_query_t,
    w_keyval,
    cosine,
    sine,
    gate_up,
    down,
    q_out,
    kv_out,
    packed,
    staged,
    sems,
):
    core = core_ref[0]
    depth, quarter = D // 2, FF // 4
    copies = [
        pltpu.make_async_copy(
            gate_up.at[pl.ds(core * depth, depth), :], staged.at[pl.ds(0, depth), :], sems.at[0]
        )
    ]
    for block in range(D // FF):
        copies.append(
            pltpu.make_async_copy(
                down.at[pl.ds(core * quarter, quarter), pl.ds(block * FF, FF)],
                staged.at[pl.ds(depth + block * quarter, quarter), :],
                sems.at[block + 1],
            )
        )
    for copy in copies:
        copy.start()
    leave = pltpu.make_async_copy(staged, packed, sems.at[4])
    x = rows[...]
    wq = w_query_t[...]
    wkv = w_keyval[...]
    src, dst = iota((128, 192), 1), iota((128, 192), 0)
    ksrc, kdst = iota((128, 128), 0), iota((128, 128), 1)

    def turned(source, target, base):
        first = (target < 32) & (source == base + target + 32)
        second = (target >= 32) & (target < 64) & (source == base + target - 32)
        return jnp.where(first, -1.0, jnp.where(second, 1.0, 0.0)).astype(BF16)

    cos, sin = cosine[...], sine[...]
    for h in range(3):
        plain = ones_where((dst < HD) & (src == h * HD + dst))
        straight = dot_t(x, dot(plain, wq).astype(BF16))
        crossed = dot_t(x, dot(turned(src, dst, h * HD), wq).astype(BF16))
        q_out[pl.ds(h * SMAX, SMAX), :] = (straight * cos + crossed * sin).astype(BF16)
        if h == 0:
            for copy in copies:
                copy.wait()
            leave.start()
    straight = dot(x, wkv)
    crossed = dot(x, dot(wkv, turned(ksrc, kdst, 0)).astype(BF16))
    kv_out[...] = (straight * cos + crossed * sin).astype(BF16)
    leave.wait()


def attend_body(
    lane_ref, core_ref, lengths, q_ref, kv_ref, prefix_ref, w_out, mine_out, other_out
):
    length, core = lengths[lane_ref[0]], core_ref[0]
    kv = kv_ref[...]
    prefix = prefix_ref[...]
    dims = (((1,), (1,)), ((), ()))
    key_at = iota((SMAX, SMAX), 1)
    keep = (key_at <= iota((SMAX, SMAX), 0)) & (key_at < length)
    heads = []
    for h in range(3):
        q = q_ref[pl.ds(h * SMAX, SMAX), :] * jnp.asarray(0.125, BF16)
        far = lax.dot_general(q, prefix, dims, preferred_element_type=F32)
        near = lax.dot_general(q, kv, dims, preferred_element_type=F32)
        near = jnp.where(keep, near, -1e30)
        top = jnp.maximum(
            jnp.max(far, axis=-1, keepdims=True), jnp.max(near, axis=-1, keepdims=True)
        )
        far = jnp.exp(far - top)
        near = jnp.where(keep, jnp.exp(near - top), 0.0)
        total = jnp.sum(far, axis=-1, keepdims=True) + jnp.sum(near, axis=-1, keepdims=True)
        mixed = dot(far.astype(BF16), prefix) + dot(near.astype(BF16), kv)
        heads.append((mixed / total)[:, HD:].astype(BF16))
    partial = dot(jnp.concatenate(heads, axis=1), w_out[...])
    partial = partial.reshape(4, 2, ROWS, D)
    first = core == 0
    mine_out[...] = jnp.where(first, partial[:, 0], partial[:, 1])
    other_out[...] = jnp.where(first, partial[:, 1], partial[:, 0]).astype(BF16)


def add_body(a, b, out):
    out[...] = (a[...] + b[...].astype(F32)).astype(BF16)


def shuffle_matrix(transposed):
    n = 4 * REM * CHUNKS
    i = iota((n, n), 1 if transposed else 0)
    j = iota((n, n), 0 if transposed else 1)
    per = REM * CHUNKS
    same = (i % (4 * REM)) // REM == j // per
    return ones_where(same & (j % per == REM * (i // (4 * REM)) + i % REM))


def pack(main, rest, out):
    for c in range(CHUNKS):
        part = main[:, c * 128 : (c + 1) * 128].reshape(EXPERTS, MAIN, 128)
        out[:, c * MAIN : (c + 1) * MAIN, :] = part.astype(BF16)
    shuffle = shuffle_matrix(True)
    for g in range(EXPERTS // 4):
        block = rest[g * 8 : (g + 1) * 8, :]
        stacked = jnp.concatenate(
            [block[:, c * 128 : (c + 1) * 128] for c in range(CHUNKS)], axis=0
        ).astype(BF16)
        units = dot(shuffle, stacked).reshape(4, REM * CHUNKS, 128)
        out[g * 4 : (g + 1) * 4, CHUNKS * MAIN :, :] = units.astype(BF16)


def unpack(units_ref, rows_ref):
    for c in range(CHUNKS):
        part = units_ref[:, c * MAIN : (c + 1) * MAIN, :].astype(F32)
        rows_ref[0 : EXPERTS * MAIN, c * 128 : (c + 1) * 128] = part.reshape(
            EXPERTS * MAIN, 128
        ).astype(BF16)
    shuffle = shuffle_matrix(False)
    gathered = []
    for g in range(EXPERTS // 4):
        units = units_ref[g * 4 : (g + 1) * 4, CHUNKS * MAIN :, :].astype(F32)
        gathered.append(dot(shuffle, units.reshape(4 * REM * CHUNKS, 128).astype(BF16)))
    for c in range(CHUNKS):
        part = jnp.concatenate([rows[c * 8 : (c + 1) * 8] for rows in gathered], axis=0)
        rows_ref[EXPERTS * MAIN :, c * 128 : (c + 1) * 128] = part.astype(BF16)


def place_of(index):
    expert = jnp.where(index < EXPERTS * MAIN, index // MAIN, (index - EXPERTS * MAIN) // REM)
    turn = jnp.where(index < EXPERTS * MAIN, index % MAIN, MAIN + index % REM)
    return expert, turn


def picks(routes_t):
    expert = expert_at(iota((EXPERTS, ROWS), 0))
    named = jnp.zeros((EXPERTS, ROWS), F32)
    for k in range(TOPK):
        named = named + ones_where(routes_t[k : k + 1, :] == expert, F32)
    named = named.astype(BF16)
    earlier = ones_where(iota((ROWS, ROWS), 0) < iota((ROWS, ROWS), 1))
    turn_of = dot(named, earlier).astype(BF16)
    total = EXPERTS * CAP
    owner, turn = place_of(iota((total, EXPERTS), 0))
    spread = ones_where(owner == iota((total, EXPERTS), 1))
    turn = turn[:, :1].astype(F32)
    return spread, (dot(spread, named) > 0.5) & (dot(spread, turn_of) == turn)


def dispatch_body(parts, states, gain, routes_t, resid_out, out):
    residual = states[...].astype(F32) + jnp.sum(parts[...].astype(F32), axis=0)
    resid_out[...] = residual
    normed = rms(residual, gain[...].astype(F32)[None]).astype(BF16)
    spread, mask = picks(routes_t)
    sent = dot(ones_where(mask), normed)
    pack(sent[: EXPERTS * MAIN], sent[EXPERTS * MAIN :], out)


def expert_body(
    core_ref, units, gate_up, down, mine_far, other_far, out, rows, mine, other, sems
):
    fetches = [
        pltpu.make_async_copy(mine_far, mine, sems.at[0]),
        pltpu.make_async_copy(other_far, other, sems.at[1]),
    ]
    for fetch in fetches:
        fetch.start()
    unpack(units, rows)
    half = FF // 2
    quarter = half // 2

    def hidden(pair):
        gate = pair[:, :half]
        return (gate * jax.nn.sigmoid(gate) * pair[:, half:]).astype(BF16)

    result = dot(hidden(dot(rows[...], gate_up[...])), down[...])
    depth = D // 2
    core = core_ref[0]
    for fetch in fetches:
        fetch.wait()
    near_rows = rows[:, pl.ds(pl.multiple_of(core * depth, 128), depth)]
    far_rows = rows[:, pl.ds(pl.multiple_of((1 - core) * depth, 128), depth)]
    inner = hidden(dot(near_rows, mine[0:depth, :]) + dot(far_rows, other[0:depth, :]))
    low, high = inner[:, :quarter], inner[:, quarter:]
    own = jnp.where(core == 0, low, high)
    rest = jnp.where(core == 0, high, low)
    parts = []
    for block in range(D // FF):
        at = pl.ds(depth + block * quarter, quarter)
        parts.append(dot(own, mine[at, :]) + dot(rest, other[at, :]))
    result = result + jnp.concatenate(parts, axis=1)
    pack(result[: EXPERTS * MAIN], result[EXPERTS * MAIN :], out)


def combine_body(lane_ref, first_ref, lengths, units, routes_t, gates_t, residual, out, rows):
    length, first = lengths[lane_ref[0]], first_ref[0]
    unpack(units, rows)
    spread, mask = picks(routes_t)
    expert = expert_at(iota((EXPERTS, ROWS), 0))
    weight = jnp.zeros((EXPERTS, ROWS), F32)
    for k in range(TOPK):
        weight = jnp.where(routes_t[k : k + 1, :] == expert, gates_t[k : k + 1, :], weight)
    high = weight.astype(BF16)
    left = weight - high.astype(F32)
    middle = left.astype(BF16)
    low = (left - middle.astype(F32)).astype(BF16)
    placed = [jnp.where(mask, dot(spread, term), 0.0) for term in (low, middle, high)]
    placed = jnp.concatenate(placed, axis=1).T.astype(BF16)
    sums = dot(placed, rows[...])
    blend = sums[0:ROWS] + sums[ROWS : 2 * ROWS] + sums[2 * ROWS :]
    live = first + iota((ROWS, 1), 0) < length
    out[...] = jnp.where(live, residual[...] + blend, 0.0).astype(BF16)


def on_device(
    states,
    gain_attn,
    gain_moe,
    w_query,
    w_keyval,
    w_out,
    prefix_cache,
    w_gate_up,
    w_down,
    routes,
    gates,
    lengths,
    group_of,
    owners,
):
    req = ("x", "yh", "z1", "z0")
    lane = lax.axis_index(req).astype(jnp.int32)
    row = (lax.axis_index(("yh", "z1")) * 2).astype(jnp.int32)[None]
    core = lax.axis_index("c").astype(jnp.int32)[None]
    first = (lax.axis_index(("l1", "l0", "c")) * ROWS).astype(jnp.int32)[None]
    lane = lane[None]
    local = states[0]
    routes_t, gates_t = routes[0].T, gates[0].T
    cosine, sine = rotary_tables()
    shape = pltpu.VMEM
    swap = [(0, 1), (1, 0)]
    hold = lax.optimization_barrier

    with jax.named_scope("norm_attn"):
        normed, copies = call(
            norm_body, (shape((ROWS, D), BF16), shape((64, 16, 128), BF16)), 3, far=(0, 1, 2)
        )(stay(local), stay(gain_attn), stay(prefix_cache[0]))
    with jax.named_scope("prefix_slices"):
        held = lax.all_to_all(copies, req, 0, 0, tiled=True)
    with jax.named_scope("gather_rows"):
        weights = [near(x) for x in (w_query.T, w_keyval, jnp.asarray(cosine), jnp.asarray(sine))]
        normed, w_out_near, *weights = hold((normed, near(w_out), *weights))
        gathered = lax.all_gather(normed, ("l1", "l0", "c"), axis=0, tiled=True)
    with jax.named_scope("prefix_deliver"):
        held, gathered, first = hold((held, gathered, first))
        chosen = call(select_body, shape((8, PIECES, 16, 128), BF16), 4, smem=(0, 1, 2))(
            row, owners, group_of, held
        )
        prefix = lax.all_to_all(chosen, ("x", "z0"), 0, 0, tiled=True).reshape(PLEN, 128)
    with jax.named_scope("project"):
        plain = jax.ShapeDtypeStruct
        queries, keyvals, packed = pl.pallas_call(
            qkv_body,
            out_shape=(
                plain((3 * SMAX, 128), BF16),
                plain((SMAX, 128), BF16),
                plain((D // 2 + FF // 4 * (D // FF), FF), BF16),
            ),
            in_specs=[SM] + [VM] * 5 + [HB, HB],
            out_specs=(VM, VM, HB),
            scratch_shapes=[
                pltpu.VMEM((D // 2 + FF // 4 * (D // FF), FF), BF16),
                pltpu.SemaphoreType.DMA((5,)),
            ],
            compiler_params=pltpu.CompilerParams(vmem_limit_bytes=24 * 2**20),
        )(
            core,
            near(gathered),
            *weights,
            stay(w_gate_up[0]),
            stay(w_down[0]),
        )
    with jax.named_scope("attend"):
        half_mine = lax.ppermute(packed, "z0", swap)
        mine, other = pl.pallas_call(
            attend_body,
            out_shape=(shape((4, ROWS, D), F32), shape((4, ROWS, D), BF16)),
            in_specs=[SM, SM, SM, VM, VM, VM, VM],
            out_specs=(VM, VM),
            compiler_params=pltpu.CompilerParams(vmem_limit_bytes=24 * 2**20),
        )(lane, core, lengths, queries, keyvals, near(prefix), w_out_near)
    with jax.named_scope("sum_heads"):
        other = lax.ppermute(other, "c", swap)
        both = call(add_body, shape((4, ROWS, D), BF16), 2)(mine, other)
        parts = lax.all_to_all(both, ("l1", "l0"), 0, 0, tiled=True)
    with jax.named_scope("dispatch"):
        residual, outbound = call(
            dispatch_body,
            (shape((ROWS, D), F32), jax.ShapeDtypeStruct((EXPERTS, UNITS, 128), BF16)),
            4,
        )(parts, local, gain_moe, routes_t)
        half_other = lax.ppermute(half_mine, "c", swap)
        inbound = exchange(outbound)
    with jax.named_scope("experts"):
        packed_shape = (D // 2 + FF // 4 * (D // FF), FF)
        produced = pl.pallas_call(
            expert_body,
            out_shape=shape((EXPERTS, UNITS, 128), BF16),
            in_specs=[SM, VM, VM, VM, HB, HB],
            out_specs=VM,
            scratch_shapes=[
                pltpu.VMEM((EXPERTS * CAP, D), BF16),
                pltpu.VMEM(packed_shape, BF16),
                pltpu.VMEM(packed_shape, BF16),
                pltpu.SemaphoreType.DMA((2,)),
            ],
            compiler_params=pltpu.CompilerParams(vmem_limit_bytes=24 * 2**20),
        )(
            core,
            near(inbound),
            near(w_gate_up[0]),
            near(w_down[0]),
            stay(half_mine),
            stay(half_other),
        )
        returned = exchange(produced)
    with jax.named_scope("combine"):
        final = call(
            combine_body,
            jax.ShapeDtypeStruct((ROWS, D), BF16),
            7,
            smem=(0, 1, 2),
            scratch=(pltpu.VMEM((EXPERTS * CAP, D), BF16),),
        )(lane, first, lengths, returned, routes_t, gates_t, residual)
    return final[None]


def solution(mesh):
    fine = Mesh(
        mesh.devices.reshape(4, 2, 4, 2, 2, 2, 2), ("x", "yh", "z1", "z0", "l1", "l0", "c")
    )
    req, tp = ("x", "yh", "z1", "z0"), ("l1", "l0", "c")
    placed = (
        P(req, tp, None),
        P(),
        P(),
        P(None, tp),
        P(None, tp),
        P(tp, None),
        P(req, None, tp),
        P(req, None, None),
        P(req, None, None),
        P(req, tp, None),
        P(req, tp, None),
        P(),
        P(),
        P(),
    )
    return jax.shard_map(
        on_device, mesh=fine, in_specs=placed, out_specs=P(req, tp, None), check_vma=False
    )
```
